256 devices in a mesh: ctx: 8 (over z_hi, core), exp: 32 (over x, z_lo, y).
Axes of the slice: x: 4, y: 4, z: 8 (z_hi: 4, z_lo: 2; z = z_hi * 2 + z_lo), core: 2. Of those that a mesh axis runs over, the one named last changes fastest.
Arguments:
- queries: bfloat16 [4096, 4096], P('ctx', 'exp'), may hold values from -8 to 8
- doc_keys: bfloat16 [8192, 4096], P('ctx', 'exp'), may hold values from -8 to 8
- doc_values: bfloat16 [8192, 4096], P('ctx', 'exp'), may hold values from -6 to 6
- residual: bfloat16 [4096, 4096], P(('ctx', 'exp')), may hold values from -3 to 3
- out_weight: bfloat16 [4096, 4096], P('exp'), may hold values from -0.09375 to 0.09375
- norm_gain: float32 [4096], replicated, may hold values from 0.1 to 1.9
- expert_ids: int32 [4096, 1], P(('ctx', 'exp')), may hold values from 0 to 7; in each aligned block of 16 rows (0 to 15, 16 to 31, ...) at most 4 rows name the same one
- gate_up: bfloat16 [32, 4096, 5120], P('exp', None, 'ctx'), may hold values from -0.09375 to 0.09375
- down_weight: bfloat16 [32, 2560, 4096], P('exp', 'ctx'), may hold values from -0.0625 to 0.0625
Outputs:
- attended: bfloat16 [4096, 4096], P(('ctx', 'exp'))
- expert_out: bfloat16 [4096, 4096], P(('ctx', 'exp'))
The draws below stay inside these ranges and needn't reach their ends.
Inputs may be any that keep to these rules, and one draw needn't show every extreme that they name: `expert_ids`: in each aligned block of 16 tokens, the rows of one device, no expert is named more than 4 times.
All inputs are finite; a program needn't handle non-finite values.
Results may differ from the reference program's by a relative error of at most 0.033.
Values may be sent and summed in bfloat16 or wider, within the bound.
No kernel may reach another device: no remote copies, remote signals or barrier semaphores. Data moves between devices by JAX's collectives and lax.ppermute only.
A program may use at most 128 MiB of HBM per device.

```python
import math
import jax
import jax.numpy as jnp
import numpy as np
from jax import lax

D = 4096
HEADS = 64
DH = 64
FF = 10240
QUARTERS = 4
TOKENS = 4096
DOC = 8192
EXPERTS = 8
ROWS = 16
CAP = 4
SLICE = 320
N_CTX = 8


def draw_queries(key, part):
    own_key = jax.random.fold_in(key, 11)
    values = 1.6 * jnp.clip(jax.random.normal(own_key, (TOKENS, HEADS * DH), jnp.float32), -5.0, 5.0)
    return values.astype(jnp.bfloat16)


def draw_doc_keys(key, part):
    own_key = jax.random.fold_in(key, 13)
    values = 1.6 * jnp.clip(jax.random.normal(own_key, (DOC, HEADS * DH), jnp.float32), -5.0, 5.0)
    return values.astype(jnp.bfloat16)


def draw_residual(key, part):
    own_key = jax.random.fold_in(key, 23)
    pick_column = jax.random.fold_in(own_key, 0)
    pick_value = jax.random.fold_in(own_key, 2)
    column_scale = jnp.exp(jax.random.uniform(pick_column, (D,), jnp.float32, math.log(0.1), 0.0))
    values = jnp.clip(jax.random.normal(pick_value, (TOKENS, D), jnp.float32), -3.0, 3.0) * column_scale[None, :]
    return values.astype(jnp.bfloat16)


def steps_of(key, extent, shards, smallest, high):
    level, own = 1.0, jax.random.fold_in(key, 6)
    for axis_at, blocks in shards:
        draws = jnp.exp(jax.random.uniform(jax.random.fold_in(own, axis_at), (blocks,), jnp.float32, smallest / len(shards), high / len(shards)))
        level = level * jnp.repeat(draws, extent[axis_at] // blocks).reshape([-1 if axis == axis_at else 1 for axis in range(len(extent))])
    return level


def shared_out(key, own, number, rows, count, top, bound, slope):
    order = jax.random.permutation(key, count)
    crowded, common = shares(count, rows * top, bound, slope, True), shares(count, rows * top, bound, slope, False)
    places = jnp.arange(count)

    def named(tallies, offset_by):
        used = int((tallies > 0).sum())
        fixed = max(1, used // 4)
        shifted = fixed + (places - fixed + offset_by * (used - fixed)) % max(1, count - fixed)
        return jnp.zeros((count,), jnp.int32).at[order[jnp.where(places < fixed, places, shifted)]].set(jnp.asarray(tallies, jnp.int32))

    tallies = jnp.where(number % 4 == 0, named(crowded, number // 4), named(common, number - number // 4 - 1))
    mixed = jax.random.permutation(jax.random.fold_in(own, 3), count)
    donor, sink = mixed[0:count // 2 * 2:2], mixed[1:count // 2 * 2:2]
    slack = jnp.minimum(tallies[donor] - 1, bound - tallies[sink]) // 2
    slack = jnp.where((donor == order[0]) | (sink == order[0]) | (tallies[sink] == 0), 0, jnp.maximum(slack, 0))
    shifted = jax.random.randint(jax.random.fold_in(own, 4), (count // 2,), 0, 1 << 20) % (slack + 1)
    tallies = tallies.at[donor].add(-shifted).at[sink].add(shifted)
    labels = jnp.searchsorted(jnp.cumsum(tallies), jnp.arange(rows * top), side="right").astype(jnp.int32)
    grid = labels.reshape(top, rows).T
    grid = grid[jax.random.permutation(jax.random.fold_in(own, 1), rows)]
    offset_by = jax.random.randint(jax.random.fold_in(own, 2), (rows, 1), 0, top)
    return jnp.take_along_axis(grid, (jnp.arange(top)[None, :] + offset_by) % top, axis=1)


def shares(number_of, total, bound, slope, full):
    weights = [(1 << 20) // math.isqrt(grade ** slope) + 1 for grade in range(1, number_of + 1)]
    largest = bound if full else min(bound, max(-(-total // number_of), total * weights[0] // sum(weights)))
    least = 1 if total - largest >= number_of - 1 else 0
    holding, rest = [largest] + [least] * (number_of - 1), total - largest - least * (number_of - 1)
    while rest > 0:
        free = [i for i in range(1, number_of) if holding[i] < largest] or [i for i in range(1, number_of) if holding[i] < bound]
        mass, left = sum([weights[i] for i in free]), rest
        for i in free:
            addition = min(bound - holding[i], max(1, left * weights[i] // mass), rest)
            holding[i] = holding[i] + addition
            rest = rest - addition
    return np.array(holding)


def scatter_about(stream_key, dims, scale, bound, shards=(), kind=jnp.bfloat16):
    values = scale * jax.random.normal(stream_key, dims, jnp.float32)
    if shards:
        values = values * steps_of(stream_key, dims, shards, -0.22, 0.18)
    return jnp.clip(values, -bound, bound).astype(kind)


def setup_inputs(seed: int = 0) -> dict:
    seeds = jax.random.split(jax.random.key(seed), 10)
    queries = draw_queries(jax.random.fold_in(seeds[9], 71), 0)
    doc_keys = draw_doc_keys(jax.random.fold_in(seeds[9], 71), 0)
    doc_values = scatter_about(seeds[2], (DOC, HEADS * DH), 1.0, 6.0, ((0, 8), (1, 32)))
    residual = draw_residual(jax.random.fold_in(seeds[9], 71), 0)
    out_weight = scatter_about(seeds[4], (HEADS * DH, D), (HEADS * DH) ** -0.5, 0.09375, ((0, 32),))
    norm_gain = jnp.clip(1.0 + 0.18 * jax.random.normal(seeds[5], (D,), jnp.float32), 0.1, 1.9)
    expert_ids_keys = jax.random.split(jax.random.fold_in(seeds[6], 1), TOKENS // ROWS)
    expert_ids_turns = jax.random.permutation(jax.random.fold_in(seeds[6], 3), TOKENS // ROWS)
    expert_ids = jax.vmap(lambda own, number: shared_out(jax.random.fold_in(seeds[6], 2), own, number, ROWS, EXPERTS, 1, CAP, 2))(expert_ids_keys, expert_ids_turns).reshape((TOKENS, 1))
    gate_up = scatter_about(seeds[7], (EXPERTS * QUARTERS, D, 2 * FF // QUARTERS), D ** -0.5, 0.09375, ((0, 32), (2, 8)))
    down_weight = scatter_about(seeds[8], (EXPERTS * QUARTERS, FF // QUARTERS, D), FF ** -0.5, 0.0625, ((0, 32), (1, 8)))
    return {"queries": queries, "doc_keys": doc_keys, "doc_values": doc_values, "residual": residual, "out_weight": out_weight, "norm_gain": norm_gain, "expert_ids": expert_ids, "gate_up": gate_up, "down_weight": down_weight}


block_rows = 128

def attend_head(operands):
    query_head, key_head, value_head = operands
    scores = jnp.dot(query_head, key_head.T, preferred_element_type=jnp.float32) * DH ** (-0.5)
    row_top = lax.optimization_barrier(jnp.max(scores, axis=1, keepdims=True))
    weights = jnp.exp(scores - row_top)
    row_total = lax.optimization_barrier(jnp.sum(weights, axis=1, keepdims=True))
    weighted = jnp.dot(weights.astype(jnp.bfloat16), value_head, preferred_element_type=jnp.float32)
    return (weighted / row_total).astype(jnp.bfloat16)

def expert_layer(normed, routes, gate_up, down_weight):
    sorted_rows = jnp.argsort(routes, stable=True).astype(jnp.int32)
    expert_range = jnp.arange(EXPERTS, dtype=jnp.int32)
    counts = lax.optimization_barrier(jnp.sum((routes[None, :] == expert_range[:, None]).astype(jnp.int32), axis=1))
    first_row = jnp.cumsum(counts) - counts
    block_count = (counts + block_rows - 1) // block_rows
    block_end = jnp.cumsum(block_count)
    block_first = block_end - block_count
    weights_in = gate_up.reshape(EXPERTS, QUARTERS, D, N_CTX, 2, SLICE)
    weights_out = down_weight.reshape(EXPERTS, QUARTERS, N_CTX, SLICE, D)
    within = jnp.arange(block_rows, dtype=jnp.int32)

    def one_block(running, block_index):
        expert = jnp.minimum(jnp.sum((block_index >= block_end).astype(jnp.int32)), EXPERTS - 1)
        local_rows = (block_index - block_first[expert]) * block_rows + within
        usable = (local_rows < counts[expert]) & (block_index < block_end[EXPERTS - 1])
        position = jnp.minimum(first_row[expert] + local_rows, TOKENS - 1).astype(jnp.int32)
        token_rows = sorted_rows[position]
        inputs = normed[token_rows].astype(jnp.float32)
        gate_up_rows = jnp.einsum('td,qdcgs->tqcgs', inputs, weights_in[expert].astype(jnp.float32), precision=lax.Precision.HIGHEST)
        hidden = lax.optimization_barrier((jax.nn.silu(gate_up_rows[:, :, :, 0]) * gate_up_rows[:, :, :, 1]).astype(jnp.bfloat16))
        pieces = jnp.einsum('tqcs,qcsd->tqcd', hidden.astype(jnp.float32), weights_out[expert].astype(jnp.float32), precision=lax.Precision.HIGHEST)
        rounded = lax.optimization_barrier(pieces.astype(jnp.bfloat16))
        summed = lax.optimization_barrier(jnp.sum(rounded.astype(jnp.float32), axis=(1, 2)))
        summed = jnp.where(usable[:, None], summed, jnp.zeros_like(summed))
        return (running.at[token_rows].add(summed), None)
    block_total = (TOKENS + block_rows - 1) // block_rows + EXPERTS
    running, ignored = lax.scan(one_block, jnp.zeros((TOKENS, D), jnp.float32), jnp.arange(block_total, dtype=jnp.int32))
    return running.astype(jnp.bfloat16)

def reference(queries, doc_keys, doc_values, residual, out_weight, norm_gain, expert_ids, gate_up, down_weight):
    query_heads = queries.reshape(TOKENS, HEADS, DH).transpose(1, 0, 2)
    key_heads = doc_keys.reshape(DOC, HEADS, DH).transpose(1, 0, 2)
    value_heads = doc_values.reshape(DOC, HEADS, DH).transpose(1, 0, 2)
    context = lax.map(attend_head, (query_heads, key_heads, value_heads))
    context = context.transpose(1, 0, 2).reshape(TOKENS, HEADS * DH)
    mixed_heads = jnp.dot(context, out_weight, preferred_element_type=jnp.float32)
    attended = lax.optimization_barrier((residual.astype(jnp.float32) + mixed_heads).astype(jnp.bfloat16))
    widened = attended.astype(jnp.float32)
    normed = (widened * lax.rsqrt(lax.optimization_barrier(jnp.mean(widened * widened, axis=1, keepdims=True)) + 1e-06) * norm_gain).astype(jnp.bfloat16)
    expert_out = expert_layer(normed, expert_ids[:, 0], gate_up, down_weight)
    return (attended, expert_out)
```

```python
import functools

import jax
import jax.numpy as jnp
from jax import lax
from jax.experimental import pallas as pl
from jax.experimental.pallas import tpu as pltpu
from jax.sharding import Mesh
from jax.sharding import PartitionSpec as P

DH = 64
QUARTERS = 4
CAP = 4
CTX = ("zhi", "core")
EXP = ("x", "zlo", "y")
PLANE = ("zhi", "zlo", "x")
INTERPRET = False


def shift(value, axis, step):
    size = lax.axis_size(axis)
    return lax.ppermute(value, axis, [(i, (i + step) % size) for i in range(size)])


def swap(value):
    return shift(value, "core", 1)


def attend_kernel(count, first, last, *refs):
    q_ref, keys, values = refs[0], refs[1 : 1 + count], refs[1 + count : 1 + 2 * count]
    rest = refs[1 + 2 * count :]
    if not first:
        acc_in, top_in, total_in = rest[:3]
        rest = rest[3:]
    head = pl.program_id(1)
    queries = q_ref[...]
    mine = lax.broadcasted_iota(jnp.int32, queries.shape, 1) // DH == head
    own = jnp.where(mine, queries, jnp.zeros_like(queries)) * jnp.asarray(DH**-0.5, queries.dtype)
    if first:
        top = jnp.full((queries.shape[0], 1), -jnp.inf, jnp.float32)
        total = jnp.zeros((queries.shape[0], 1), jnp.float32)
        acc = jnp.zeros(queries.shape, jnp.float32)
    else:
        top = jnp.max(jnp.where(mine, top_in[...], -jnp.inf), axis=1, keepdims=True)
        total = jnp.max(jnp.where(mine, total_in[...], 0.0), axis=1, keepdims=True)
        acc = acc_in[...]
    for block in range(count):
        scores = lax.dot_general(
            own, keys[block][...], (((1,), (1,)), ((), ())), preferred_element_type=jnp.float32
        )
        new_top = jnp.maximum(top, jnp.max(scores, axis=1, keepdims=True))
        decay = jnp.exp(top - new_top)
        weights = jnp.exp(scores - new_top)
        total = total * decay + jnp.sum(weights, axis=1, keepdims=True)
        acc = acc * decay + jnp.dot(
            weights.astype(jnp.bfloat16), values[block][...], preferred_element_type=jnp.float32
        )
        top = new_top
    if last:
        results = ((acc / total).astype(jnp.bfloat16),)
    else:
        results = (acc, jnp.broadcast_to(top, acc.shape), jnp.broadcast_to(total, acc.shape))

    @pl.when(head == 0)
    def _():
        for ref, result in zip(rest, results):
            ref[...] = result

    @pl.when(head != 0)
    def _():
        for ref, result in zip(rest, results):
            ref[...] = jnp.where(mine, result, ref[...])


def attend(queries, keys, values, state, last, name):
    total_rows, width = queries.shape
    rows = min(256, total_rows)
    count = len(keys)
    heads = width // DH
    whole = [pl.BlockSpec(k.shape, lambda i, h: (0, 0)) for k in keys + values]
    part = pl.BlockSpec((rows, width), lambda i, h: (i, 0))
    docs = sum(k.shape[0] for k in keys)
    if last:
        shapes = [jax.ShapeDtypeStruct(queries.shape, jnp.bfloat16)]
    else:
        shapes = [jax.ShapeDtypeStruct(queries.shape, jnp.float32)] * 3
    return pl.pallas_call(
        functools.partial(attend_kernel, count, not state, last),
        grid=(total_rows // rows, heads),
        in_specs=[part] + whole + [part] * len(state),
        out_specs=[part] * len(shapes),
        out_shape=shapes,
        cost_estimate=pl.CostEstimate(
            flops=4 * total_rows * docs * width,
            bytes_accessed=4 * docs * width + 14 * total_rows * width,
            transcendentals=heads * total_rows * docs,
        ),
        name=name,
        interpret=INTERPRET,
    )(queries, *keys, *values, *state)


def attention(queries, keys, values, early):
    keys_c, values_c = swap(keys), swap(values)
    keys_p, keys_m = shift(keys, "zhi", 1), shift(keys, "zhi", -1)
    values_p, values_m = shift(values, "zhi", 1), shift(values, "zhi", -1)
    state = attend(queries, [keys, keys_c], [values, values_c], [], False, "attend_own")
    state, keys_p, keys_m, values_p, values_m, early = lax.optimization_barrier(
        (state, keys_p, keys_m, values_p, values_m, early)
    )
    keys_2, values_2 = shift(keys_p, "zhi", 1), shift(values_m, "zhi", -1)
    state = attend(
        queries,
        [keys_p, keys_m, swap(keys_p), swap(keys_m)],
        [values_p, values_m, swap(values_p), swap(values_m)],
        state,
        False,
        "attend_side",
    )
    state, keys_2, values_2 = lax.optimization_barrier((state, keys_2, values_2))
    (context,) = attend(
        queries, [keys_2, swap(keys_2)], [values_2, swap(values_2)], state, True, "attend_far"
    )
    return context, early


def expert_block(own, other, gate_up, down_weight):
    slice_width = down_weight.shape[0]
    rows = jnp.concatenate([own, other], axis=0)
    gate_and_up = jnp.dot(rows, gate_up, preferred_element_type=jnp.float32)
    hidden = (jax.nn.silu(gate_and_up[:, :slice_width]) * gate_and_up[:, slice_width:]).astype(jnp.bfloat16)
    half = own.shape[0]
    out_other = jnp.dot(hidden[half:], down_weight, preferred_element_type=jnp.float32).astype(jnp.bfloat16)
    out_own = jnp.dot(hidden[:half], down_weight, preferred_element_type=jnp.float32)
    return (out_own + swap(out_other).astype(jnp.float32)).astype(jnp.bfloat16)


def add_rounded(a, b):
    return (a.astype(jnp.float32) + b.astype(jnp.float32)).astype(jnp.bfloat16)


def slot_choice(routes, nx, nzlo, rows):
    positions = jnp.arange(rows, dtype=jnp.int32)
    earlier = (routes[:, :, None] == routes[:, None, :]) & (positions[:, None] > positions[None, :])
    rank = jnp.sum(earlier.astype(jnp.int32), axis=2)
    expert_of = (
        jnp.arange(nx, dtype=jnp.int32)[None, :] * nzlo + jnp.arange(nzlo, dtype=jnp.int32)[:, None]
    ).reshape(-1)
    slots = jnp.arange(CAP, dtype=jnp.int32)
    blocks = jnp.arange(nx, dtype=jnp.int32)
    chosen = (
        (routes[None, None, None, :, :] == expert_of[:, None, None, None, None])
        & (rank[None, None, None, :, :] == slots[None, None, :, None, None])
        & (blocks[None, :, None, None, None] == blocks[None, None, None, :, None])
    )
    chosen = chosen.reshape(nx * nzlo * nx * CAP, nx * rows).astype(jnp.bfloat16)
    return chosen, expert_of, positions, slots


def on_device(
    queries, doc_keys, doc_values, residual, out_weight, norm_gain, expert_ids, gate_up, down_weight
):
    nx, nzlo, ny, nzhi = (lax.axis_size(a) for a in ("x", "zlo", "y", "zhi"))
    rows, width = residual.shape
    chunk = width // nx
    group = nzlo * ny
    experts = nx * nzlo

    ordered = queries.reshape(nx, group, rows, -1).transpose(1, 0, 2, 3).reshape(queries.shape)
    weight_chunk = lax.all_to_all(out_weight, "x", split_axis=1, concat_axis=0, tiled=True)
    residual_chunk = lax.all_to_all(residual, "x", split_axis=1, concat_axis=0, tiled=True)
    routes = lax.all_gather(expert_ids[:, 0], "x", axis=0, tiled=False)
    chosen, expert_of, positions, slots = slot_choice(routes, nx, nzlo, rows)
    context, (weight_chunk, residual_chunk, chosen) = attention(
        ordered, doc_keys, doc_values, (weight_chunk, residual_chunk, chosen)
    )
    contexts = lax.all_gather(context, "x", axis=1, tiled=True)
    partial_rows = jnp.dot(contexts, weight_chunk, preferred_element_type=jnp.float32).astype(jnp.bfloat16)
    pieces = lax.all_to_all(
        partial_rows.reshape(group, nx * rows, chunk), ("zlo", "y"), split_axis=0, concat_axis=0, tiled=True
    )
    mixed = jnp.sum(pieces.astype(jnp.float32), axis=0)
    attended_chunk = (residual_chunk.astype(jnp.float32) + mixed).astype(jnp.bfloat16)
    attended = lax.all_to_all(attended_chunk, "x", split_axis=0, concat_axis=1, tiled=True)

    outgoing = jnp.dot(chosen, attended_chunk, preferred_element_type=jnp.float32).astype(jnp.bfloat16)
    outgoing = outgoing.reshape(1, experts, nx * CAP, chunk)
    outgoing = jnp.broadcast_to(outgoing, (nzhi,) + outgoing.shape[1:]).reshape(
        nzhi * experts, nx * CAP, chunk
    )
    incoming = lax.all_to_all(outgoing, PLANE, split_axis=0, concat_axis=0, tiled=True)
    incoming = incoming.reshape(nzhi * nzlo, nx, nx * CAP, chunk).transpose(0, 2, 1, 3)
    widened = incoming.reshape(nzhi * nzlo * nx * CAP, width).astype(jnp.float32)
    normed = (
        widened * lax.rsqrt(jnp.mean(widened * widened, axis=1, keepdims=True) + 1e-06) * norm_gain
    ).astype(jnp.bfloat16)

    half = normed.shape[0] // 2
    from_prev, from_next = shift(normed, "y", 1), shift(normed, "y", -1)
    far = jnp.concatenate(
        [shift(from_prev[:half], "y", 1), shift(from_next[half:], "y", -1)], axis=0
    )
    gate_up, down_weight = gate_up[0], down_weight[0]
    sum_own = expert_block(normed, swap(normed), gate_up, down_weight)
    sum_prev = expert_block(from_prev, swap(from_prev), gate_up, down_weight)
    sum_next = expert_block(from_next, swap(from_next), gate_up, down_weight)
    sum_far = expert_block(far, swap(far), gate_up, down_weight)
    relay_next = shift(sum_far[:half], "y", 1)
    relay_prev = shift(sum_far[half:], "y", -1)
    to_next = jnp.concatenate([add_rounded(sum_next[:half], relay_next), sum_next[half:]], axis=0)
    to_prev = jnp.concatenate([sum_prev[:half], add_rounded(sum_prev[half:], relay_prev)], axis=0)
    got_prev, got_next = shift(to_next, "y", 1), shift(to_prev, "y", -1)
    summed = (
        sum_own.astype(jnp.float32) + got_prev.astype(jnp.float32) + got_next.astype(jnp.float32)
    ).astype(jnp.bfloat16)

    returned = lax.all_to_all(
        summed.reshape(nzhi * nzlo * nx, CAP, width), PLANE, split_axis=0, concat_axis=0, tiled=True
    )
    own_routes = expert_ids[:, 0]
    own_earlier = (own_routes[:, None] == own_routes[None, :]) & (positions[:, None] > positions[None, :])
    own_rank = jnp.sum(own_earlier.astype(jnp.int32), axis=1)
    picked = (own_routes[:, None, None] == expert_of[None, :, None]) & (
        own_rank[:, None, None] == slots[None, None, :]
    )
    picked = jnp.broadcast_to(picked[:, None], (rows, nzhi) + picked.shape[1:]).reshape(rows, -1)
    expert_sum = jnp.dot(
        picked.astype(jnp.bfloat16), returned.reshape(-1, width), preferred_element_type=jnp.float32
    )
    return (attended, expert_sum.astype(jnp.bfloat16))


def solution(mesh):
    split = Mesh(mesh.devices.reshape(4, 2, 4, 2, 4), CTX + EXP)
    return jax.shard_map(
        on_device,
        mesh=split,
        in_specs=(
            P(CTX, EXP),
            P(CTX, EXP),
            P(CTX, EXP),
            P(CTX + EXP, None),
            P(EXP, None),
            P(),
            P(CTX + EXP, None),
            P(EXP, None, CTX),
            P(EXP, CTX, None),
        ),
        out_specs=(P(CTX + EXP, None), P(CTX + EXP, None)),
        check_vma=False,
    )
```

```python
import functools

import jax
import jax.numpy as jnp
from jax import lax
from jax.experimental import pallas as pl
from jax.sharding import Mesh
from jax.sharding import PartitionSpec as P

DH = 64
CAP = 4
CTX = ("zhi", "core")
EXP = ("x", "zlo", "y")
PLANE = ("zhi", "zlo", "x")
INTERPRET = False


def shift(value, axis, step):
    size = lax.axis_size(axis)
    return lax.ppermute(value, axis, [(i, (i + step) % size) for i in range(size)])


def swap(value):
    return shift(value, "core", 1)


def attend_kernel(count, first, last, *refs):
    q_ref, blocks = refs[0], refs[1 : 1 + count]
    rest = refs[1 + count :]
    if not first:
        acc_in, top_in, total_in = rest[:3]
        rest = rest[3:]
    head = pl.program_id(1)
    queries = q_ref[...]
    width = queries.shape[1]
    mine = lax.broadcasted_iota(jnp.int32, queries.shape, 1) // DH == head
    own = jnp.where(mine, queries, jnp.zeros_like(queries)) * jnp.asarray(DH**-0.5, queries.dtype)
    if first:
        top = jnp.full((queries.shape[0], 1), -jnp.inf, jnp.float32)
        total = jnp.zeros((queries.shape[0], 1), jnp.float32)
        acc = jnp.zeros(queries.shape, jnp.float32)
    else:
        top = jnp.max(jnp.where(mine, top_in[...], -jnp.inf), axis=1, keepdims=True)
        total = jnp.max(jnp.where(mine, total_in[...], 0.0), axis=1, keepdims=True)
        acc = acc_in[...]
    for block in blocks:
        scores = lax.dot_general(
            own, block[:, :width], (((1,), (1,)), ((), ())), preferred_element_type=jnp.float32
        )
        new_top = jnp.maximum(top, jnp.max(scores, axis=1, keepdims=True))
        decay = jnp.exp(top - new_top)
        weights = jnp.exp(scores - new_top)
        total = total * decay + jnp.sum(weights, axis=1, keepdims=True)
        acc = acc * decay + jnp.dot(
            weights.astype(jnp.bfloat16), block[:, width:], preferred_element_type=jnp.float32
        )
        top = new_top
    if last:
        results = ((acc / total).astype(jnp.bfloat16),)
    else:
        results = (acc, jnp.broadcast_to(top, acc.shape), jnp.broadcast_to(total, acc.shape))

    @pl.when(head == 0)
    def _():
        for ref, result in zip(rest, results):
            ref[...] = result

    @pl.when(head != 0)
    def _():
        for ref, result in zip(rest, results):
            ref[...] = jnp.where(mine, result, ref[...])


def attend(queries, blocks, state, last):
    total_rows, width = queries.shape
    rows = min(256, total_rows)
    heads = width // DH
    whole = [pl.BlockSpec(k.shape, lambda i, h: (0, 0)) for k in blocks]
    part = pl.BlockSpec((rows, width), lambda i, h: (i, 0))
    docs = sum(k.shape[0] for k in blocks)
    if last:
        shapes = [jax.ShapeDtypeStruct(queries.shape, jnp.bfloat16)]
    else:
        shapes = [jax.ShapeDtypeStruct(queries.shape, jnp.float32)] * 3
    return pl.pallas_call(
        functools.partial(attend_kernel, len(blocks), not state, last),
        grid=(total_rows // rows, heads),
        in_specs=[part] + whole + [part] * len(state),
        out_specs=[part] * len(shapes),
        out_shape=shapes,
        cost_estimate=pl.CostEstimate(
            flops=4 * total_rows * docs * width,
            bytes_accessed=4 * docs * width + 14 * total_rows * width,
            transcendentals=heads * total_rows * docs,
        ),
        interpret=INTERPRET,
    )(queries, *blocks, *state)


def attention(queries, pairs, early):
    pairs_c = swap(pairs)
    pairs_p, pairs_m = shift(pairs, "zhi", 1), shift(pairs, "zhi", -1)
    state = attend(queries, [pairs, pairs_c], [], False)
    state, pairs_p, pairs_m = lax.optimization_barrier((state, pairs_p, pairs_m))
    half = pairs.shape[0] // 2
    far_a, far_b = shift(pairs_p[:half], "zhi", 1), shift(pairs_m[half:], "zhi", -1)
    pairs_pc, pairs_mc = swap(pairs_p), swap(pairs_m)
    state = attend(queries, [pairs_p, pairs_m], state, False)
    state = attend(queries, [pairs_pc, pairs_mc], state, False)
    state, far_a, far_b, early = lax.optimization_barrier((state, far_a, far_b, early))
    far_ac, far_bc = swap(far_a), swap(far_b)
    state = attend(queries, [far_a, far_b], state, False)
    (context,) = attend(queries, [far_ac, far_bc], state, True)
    return context, early


def project_kernel(count, *refs):
    context = jnp.concatenate([r[...] for r in refs[:count]], axis=1)
    weight = jnp.concatenate([r[...] for r in refs[count : 2 * count]], axis=0)
    refs[-1][...] = jnp.dot(context, weight, preferred_element_type=jnp.float32).astype(jnp.bfloat16)


def project(contexts, weights):
    rows, width = contexts[0].shape
    chunk = weights[0].shape[1]
    part = min(256, chunk)
    count = len(contexts)
    return pl.pallas_call(
        functools.partial(project_kernel, count),
        grid=(chunk // part,),
        in_specs=[pl.BlockSpec((rows, width), lambda i: (0, 0))] * count
        + [pl.BlockSpec((width, part), lambda i: (0, i))] * count,
        out_specs=pl.BlockSpec((rows, part), lambda i: (0, i)),
        out_shape=jax.ShapeDtypeStruct((rows, chunk), jnp.bfloat16),
        cost_estimate=pl.CostEstimate(
            flops=2 * rows * width * count * chunk,
            bytes_accessed=2 * (rows * width * count + width * count * chunk + rows * chunk),
            transcendentals=0,
        ),
        name="project",
        interpret=INTERPRET,
    )(*contexts, *weights)


def norm_kernel(groups, chunks, in_ref, gain_ref, out_ref):
    rows, chunk = in_ref.shape[1:]
    for group in range(groups):
        parts = [in_ref[group * chunks + i].astype(jnp.float32) for i in range(chunks)]
        squares = sum(jnp.sum(p * p, axis=1, keepdims=True) for p in parts)
        scale = lax.rsqrt(squares * (1.0 / (chunks * chunk)) + 1e-06)
        for i, p in enumerate(parts):
            gain = gain_ref[:, i * chunk : (i + 1) * chunk]
            out_ref[group * rows : (group + 1) * rows, i * chunk : (i + 1) * chunk] = (
                p * scale * gain
            ).astype(jnp.bfloat16)


def norm_rows(incoming, gain, groups, chunks):
    rows, chunk = incoming.shape[1:]
    shape = (groups * rows, chunks * chunk)
    return pl.pallas_call(
        functools.partial(norm_kernel, groups, chunks),
        out_shape=jax.ShapeDtypeStruct(shape, jnp.bfloat16),
        cost_estimate=pl.CostEstimate(
            flops=4 * shape[0] * shape[1], bytes_accessed=4 * shape[0] * shape[1], transcendentals=shape[0]
        ),
        name="norm_rows",
        interpret=INTERPRET,
    )(incoming, gain[None, :])


def expert_block(own, other, gate_up, down_weight):
    slice_width = down_weight.shape[0]
    half = own.shape[0]
    rows = jnp.concatenate([own, other], axis=0)
    gate_and_up = jnp.dot(rows, gate_up, preferred_element_type=jnp.float32)
    hidden = (jax.nn.silu(gate_and_up[:, :slice_width]) * gate_and_up[:, slice_width:]).astype(
        jnp.bfloat16
    )
    out_other = jnp.dot(hidden[half:], down_weight, preferred_element_type=jnp.float32)
    out_other = out_other.astype(jnp.bfloat16)
    out_own = jnp.dot(hidden[:half], down_weight, preferred_element_type=jnp.float32)
    return add_rounded(out_own, swap(out_other))


def add_rounded(a, b):
    return (a.astype(jnp.float32) + b.astype(jnp.float32)).astype(jnp.bfloat16)


def last_sum_kernel(own_ref, low_a, low_b, high_a, high_b, out_ref):
    half = low_a.shape[0]
    wide = own_ref.shape[1] // 2
    for start, first, second in ((0, low_a, low_b), (half, high_a, high_b)):
        for at in range(0, half, CAP):
            rows = slice(start + at, start + at + CAP)
            whole = (
                own_ref[rows].astype(jnp.float32)
                + first[at : at + CAP].astype(jnp.float32)
                + second[at : at + CAP].astype(jnp.float32)
            )
            both = jnp.concatenate([whole[:, :wide], whole[:, wide:]], axis=0)
            out_ref[(start + at) // CAP] = both.astype(jnp.bfloat16)


def last_sum(own, low_a, low_b, high_a, high_b):
    rows, width = own.shape
    shape = (rows // CAP, 2 * CAP, width // 2)
    return pl.pallas_call(
        last_sum_kernel,
        out_shape=jax.ShapeDtypeStruct(shape, jnp.bfloat16),
        cost_estimate=pl.CostEstimate(
            flops=2 * rows * width, bytes_accessed=8 * rows * width, transcendentals=0
        ),
        name="last_sum",
        interpret=INTERPRET,
    )(own, low_a, low_b, high_a, high_b)


def slot_choice(routes, nx, nzlo, rows):
    positions = jnp.arange(rows, dtype=jnp.int32)
    earlier = (routes[:, :, None] == routes[:, None, :]) & (positions[:, None] > positions[None, :])
    rank = jnp.sum(earlier.astype(jnp.int32), axis=2)
    expert_of = (
        jnp.arange(nx, dtype=jnp.int32)[None, :] * nzlo + jnp.arange(nzlo, dtype=jnp.int32)[:, None]
    ).reshape(-1)
    slots = jnp.arange(CAP, dtype=jnp.int32)
    blocks = jnp.arange(nx, dtype=jnp.int32)
    chosen = (
        (routes[None, None, None, :, :] == expert_of[:, None, None, None, None])
        & (rank[None, None, None, :, :] == slots[None, None, :, None, None])
        & (blocks[None, :, None, None, None] == blocks[None, None, None, :, None])
    )
    chosen = chosen.reshape(nx * nzlo * nx * CAP, nx * rows).astype(jnp.bfloat16)
    return chosen, expert_of, positions, slots


def on_device(
    queries, doc_keys, doc_values, residual, out_weight, norm_gain, expert_ids, gate_up, down_weight
):
    nx, nzlo, ny, nzhi = (lax.axis_size(a) for a in ("x", "zlo", "y", "zhi"))
    rows, width = residual.shape
    chunk = width // nx
    group = nzlo * ny
    experts = nx * nzlo

    at_x = lax.axis_index("x")

    def exchange(value):
        def chunk_of(step):
            return lax.dynamic_slice_in_dim(value, (at_x + step) % nx * chunk, chunk, axis=1)

        return [chunk_of(0)] + [shift(chunk_of(step), "x", step) for step in (1, -1, 2)]

    pairs = jnp.concatenate([doc_keys, doc_values], axis=1)
    ordered = queries.reshape(nx, group, rows, -1).transpose(1, 0, 2, 3).reshape(queries.shape)
    weight_chunks = exchange(out_weight)
    ids_column = jnp.broadcast_to(expert_ids.astype(jnp.bfloat16), (rows, 128))
    residual_parts = exchange(residual)
    ids_parts = [ids_column] + [shift(ids_column, "x", step) for step in (1, -1, 2)]
    residual_chunk = jnp.zeros((nx, rows, chunk), jnp.bfloat16)
    routes = jnp.zeros((nx, rows, 128), jnp.bfloat16)
    for part, ids, step in zip(residual_parts, ids_parts, (0, 1, -1, 2)):
        place = ((at_x - step) % nx, 0, 0)
        residual_chunk = lax.dynamic_update_slice(residual_chunk, part[None], place)
        routes = lax.dynamic_update_slice(routes, ids[None], place)
    residual_chunk = residual_chunk.reshape(nx * rows, chunk)
    routes = routes[:, :, 0].astype(jnp.int32)
    chosen, expert_of, positions, slots = slot_choice(routes, nx, nzlo, rows)
    context, (weight_chunks, residual_chunk, chosen) = attention(
        ordered, pairs, (weight_chunks, residual_chunk, chosen)
    )
    contexts = [context] + [shift(context, "x", step) for step in (1, -1, 2)]
    partial_rows = project(contexts, weight_chunks)
    pieces = lax.all_to_all(
        partial_rows.reshape(group, nx * rows, chunk), ("zlo", "y"), split_axis=0, concat_axis=0, tiled=True
    )
    mixed = jnp.sum(pieces.astype(jnp.float32), axis=0)
    attended_chunk = (residual_chunk.astype(jnp.float32) + mixed).astype(jnp.bfloat16)
    attended = lax.all_to_all(attended_chunk, "x", split_axis=0, concat_axis=1, tiled=True)

    outgoing = jnp.dot(chosen, attended_chunk, preferred_element_type=jnp.float32).astype(jnp.bfloat16)
    outgoing = outgoing.reshape(1, experts, nx * CAP, chunk)
    outgoing = jnp.broadcast_to(outgoing, (nzhi,) + outgoing.shape[1:]).reshape(
        nzhi * experts, nx * CAP, chunk
    )
    incoming = lax.all_to_all(outgoing, PLANE, split_axis=0, concat_axis=0, tiled=True)
    normed = norm_rows(incoming, norm_gain, nzhi * nzlo, nx)

    half = normed.shape[0] // 2
    gate_up, down_weight = gate_up[0], down_weight[0]
    from_prev, from_next = shift(normed, "y", 1), shift(normed, "y", -1)
    sum_own = expert_block(normed, swap(normed), gate_up, down_weight)
    far_a = shift(from_prev[:half], "y", 1)
    far_b = shift(from_next[half:], "y", -1)
    sum_prev = expert_block(from_prev, swap(from_prev), gate_up, down_weight)
    sum_next = expert_block(from_next, swap(from_next), gate_up, down_weight)
    early_next = shift(sum_next[half:], "y", 1)
    early_prev = shift(sum_prev[:half], "y", -1)
    far = jnp.concatenate([far_a, far_b], axis=0)
    sum_far = expert_block(far, swap(far), gate_up, down_weight)
    relay_next, relay_prev = shift(sum_far[:half], "y", 1), shift(sum_far[half:], "y", -1)
    late_next = shift(add_rounded(sum_next[:half], relay_next), "y", 1)
    late_prev = shift(add_rounded(sum_prev[half:], relay_prev), "y", -1)
    summed = last_sum(sum_own, late_next, early_prev, early_next, late_prev)
    returned = lax.all_to_all(summed, PLANE, split_axis=0, concat_axis=0, tiled=True)
    own_routes = expert_ids[:, 0]
    own_earlier = (own_routes[:, None] == own_routes[None, :]) & (positions[:, None] > positions[None, :])
    own_rank = jnp.sum(own_earlier.astype(jnp.int32), axis=1)
    picked = (own_routes[:, None, None] == expert_of[None, :, None]) & (
        own_rank[:, None, None] == slots[None, None, :]
    )
    halves = jnp.arange(2, dtype=jnp.int32)
    picked = (halves[:, None] == halves[None, :])[:, None, None, None, :, None] & jnp.broadcast_to(
        picked[None, :, None, :, None, :], (1, rows, nzhi, nx * nzlo, 1, CAP)
    )
    expert_sum = jnp.dot(
        picked.reshape(2 * rows, -1).astype(jnp.bfloat16),
        returned.reshape(-1, width // 2),
        preferred_element_type=jnp.float32,
    )
    expert_sum = expert_sum.reshape(2, rows, width // 2).transpose(1, 0, 2).reshape(rows, width)
    return (attended, expert_sum.astype(jnp.bfloat16))


def solution(mesh):
    split = Mesh(mesh.devices.reshape(4, 2, 4, 2, 4), CTX + EXP)
    return jax.shard_map(
        on_device,
        mesh=split,
        in_specs=(
            P(CTX, EXP),
            P(CTX, EXP),
            P(CTX, EXP),
            P(CTX + EXP, None),
            P(EXP, None),
            P(),
            P(CTX + EXP, None),
            P(EXP, None, CTX),
            P(EXP, CTX, None),
        ),
        out_specs=(P(CTX + EXP, None), P(CTX + EXP, None)),
        check_vma=False,
    )
```

```python
import functools

import jax
import jax.numpy as jnp
from jax import lax
from jax.experimental import pallas as pl
from jax.experimental.pallas import tpu as pltpu
from jax.sharding import Mesh
from jax.sharding import PartitionSpec as P

DH = 64
CAP = 4
CTX = ("zhi", "core")
EXP = ("x", "zlo", "y")
PLANE = ("zhi", "zlo", "x")
INTERPRET = False


X_STEPS = (0, 1, -1, 2)


def shift(value, axis, step):
    size = lax.axis_size(axis)
    return lax.ppermute(value, axis, [(i, (i + step) % size) for i in range(size)])


def swap(value):
    return shift(value, "core", 1)


def in_vmem(value):
    return value if INTERPRET else pltpu.with_memory_space_constraint(value, pltpu.VMEM)


def attend_kernel(count, first, last, *refs):
    q_ref, keys, values = refs[0], refs[1 : 1 + count], refs[1 + count : 1 + 2 * count]
    rest = refs[1 + 2 * count :]
    if not first:
        acc_in, top_in, total_in = rest[:3]
        rest = rest[3:]
    head = pl.program_id(1)
    queries = q_ref[...]
    mine = lax.broadcasted_iota(jnp.int32, queries.shape, 1) // DH == head
    own = jnp.where(mine, queries, jnp.zeros_like(queries)) * jnp.asarray(DH**-0.5, queries.dtype)
    if first:
        top = jnp.full((queries.shape[0], 1), -jnp.inf, jnp.float32)
        total = jnp.zeros((queries.shape[0], 1), jnp.float32)
        acc = jnp.zeros(queries.shape, jnp.float32)
    else:
        top = jnp.max(jnp.where(mine, top_in[...], -jnp.inf), axis=1, keepdims=True)
        total = jnp.max(jnp.where(mine, total_in[...], 0.0), axis=1, keepdims=True)
        acc = acc_in[...]
    for key, value in zip(keys, values):
        scores = lax.dot_general(
            own, key[...], (((1,), (1,)), ((), ())), preferred_element_type=jnp.float32
        )
        new_top = jnp.maximum(top, jnp.max(scores, axis=1, keepdims=True))
        decay = jnp.exp(top - new_top)
        weights = jnp.exp(scores - new_top)
        total = total * decay + jnp.sum(weights, axis=1, keepdims=True)
        acc = acc * decay + jnp.dot(
            weights.astype(jnp.bfloat16), value[...], preferred_element_type=jnp.float32
        )
        top = new_top
    if last:
        results = ((acc / total).astype(jnp.bfloat16),)
    else:
        results = (acc, jnp.broadcast_to(top, acc.shape), jnp.broadcast_to(total, acc.shape))

    @pl.when(head == 0)
    def _():
        for ref, result in zip(rest, results):
            ref[...] = result

    @pl.when(head != 0)
    def _():
        for ref, result in zip(rest, results):
            ref[...] = jnp.where(mine, result, ref[...])


def attend(queries, keys, values, state, last):
    total_rows, width = queries.shape
    rows = min(256, total_rows)
    heads = width // DH
    whole = [pl.BlockSpec(k.shape, lambda i, h: (0, 0)) for k in keys + values]
    part = pl.BlockSpec((rows, width), lambda i, h: (i, 0))
    docs = sum(k.shape[0] for k in keys)
    if last:
        shapes = [jax.ShapeDtypeStruct(queries.shape, jnp.bfloat16)]
    else:
        shapes = [jax.ShapeDtypeStruct(queries.shape, jnp.float32)] * 3
    return pl.pallas_call(
        functools.partial(attend_kernel, len(keys), not state, last),
        grid=(total_rows // rows, heads),
        in_specs=[part] + whole + [part] * len(state),
        out_specs=[part] * len(shapes),
        out_shape=shapes,
        cost_estimate=pl.CostEstimate(
            flops=4 * total_rows * docs * width,
            bytes_accessed=4 * docs * width + 14 * total_rows * width,
            transcendentals=heads * total_rows * docs,
        ),
        interpret=INTERPRET,
    )(queries, *keys, *values, *state)


def attention(queries, keys, values, early):
    near_keys = [swap(keys), shift(keys, "zhi", 1), shift(keys, "zhi", -1)]
    near_values = [swap(values), shift(values, "zhi", 1), shift(values, "zhi", -1)]
    state = attend(queries, [keys, near_keys[0]], [values, near_values[0]], [], False)
    far_key = shift(near_keys[1], "zhi", 1)
    far_value = shift(near_values[2], "zhi", -1)
    state = attend(
        queries,
        near_keys[1:] + [swap(k) for k in near_keys[1:]],
        near_values[1:] + [swap(v) for v in near_values[1:]],
        state,
        False,
    )
    state, far_key, far_value, early = lax.optimization_barrier((state, far_key, far_value, early))
    (context,) = attend(queries, [far_key, swap(far_key)], [far_value, swap(far_value)], state, True)
    return context, early


def pack_kernel(x_ref, residual_ref, ids_ref, weight_ref, *out_refs):
    wide, chunk = weight_ref.shape[0], weight_ref.shape[1] // len(out_refs)
    rows = residual_ref.shape[0]
    for step, out_ref in zip(X_STEPS, out_refs):
        at = pl.multiple_of((x_ref[0] + step + 4) % 4 * chunk, chunk)
        out_ref[:wide, :chunk] = weight_ref[:, pl.ds(at, chunk)]
        out_ref[:wide, chunk:] = jnp.zeros((wide, out_ref.shape[1] - chunk), jnp.bfloat16)
        out_ref[wide:, :chunk] = residual_ref[:, pl.ds(at, chunk)]
        out_ref[wide:, chunk:] = jnp.broadcast_to(
            ids_ref[...].astype(jnp.float32), (rows, out_ref.shape[1] - chunk)
        ).astype(jnp.bfloat16)


def pack(at_x, residual, ids, weight):
    nx = lax.axis_size("x")
    shape = (weight.shape[0] + residual.shape[0], weight.shape[1] // nx + 128)
    vmem = pl.BlockSpec(memory_space=pltpu.VMEM)
    return pl.pallas_call(
        pack_kernel,
        in_specs=[pl.BlockSpec(memory_space=pltpu.SMEM), vmem, vmem, vmem],
        out_shape=[jax.ShapeDtypeStruct(shape, jnp.bfloat16)] * nx,
        cost_estimate=pl.CostEstimate(
            flops=0, bytes_accessed=4 * weight.shape[0] * weight.shape[1], transcendentals=0
        ),
        name="pack",
        interpret=INTERPRET,
    )(at_x, residual, ids, weight)


def choose_kernel(nx, nzlo, x_ref, *refs):
    parts, (residual_ref, chosen_ref) = refs[:nx], refs[nx:]
    rows, chunk = parts[0].shape[0], residual_ref.shape[1]
    tokens = nx * rows
    got = jnp.concatenate([p[...].astype(jnp.float32) for p in parts], axis=0)
    row = lax.broadcasted_iota(jnp.int32, (tokens, tokens), 0)
    column = lax.broadcasted_iota(jnp.int32, (tokens, tokens), 1)
    source = jnp.zeros((tokens, tokens), jnp.int32)
    for at, step in enumerate(X_STEPS):
        source = jnp.where(row // rows == (x_ref[0] - step + 4) % 4, at * rows + row % rows, source)
    order = (column == source).astype(jnp.bfloat16)
    ordered = jnp.dot(order, got.astype(jnp.bfloat16), preferred_element_type=jnp.float32)
    residual_ref[...] = ordered[:, :chunk].astype(jnp.bfloat16)
    by_row = ordered[:, chunk : chunk + tokens]
    by_column = jnp.sum(jnp.where(row == column, by_row, 0.0), axis=0, keepdims=True)
    earlier = (by_row == by_column) & (row // rows == column // rows) & (row < column)
    rank = jnp.sum(earlier.astype(jnp.float32), axis=0, keepdims=True)
    slots = chosen_ref.shape[0]
    row = lax.broadcasted_iota(jnp.int32, (slots, tokens), 0)
    column = lax.broadcasted_iota(jnp.int32, (slots, tokens), 1)
    plane = row // (nx * CAP)
    expert = (plane % nx * nzlo + plane // nx).astype(jnp.float32)
    chosen = (
        (by_column == expert)
        & (rank == (row % CAP).astype(jnp.float32))
        & (row // CAP % nx == column // rows)
    )
    chosen_ref[...] = chosen.astype(jnp.bfloat16)


def choose(at_x, payloads, rows, chunk, nx, nzlo):
    high = payloads[0].shape[0] // rows - 1
    shapes = [(nx * rows, chunk), (nx * nzlo * nx * CAP, nx * rows)]
    return pl.pallas_call(
        functools.partial(choose_kernel, nx, nzlo),
        grid=(1,),
        in_specs=[pl.BlockSpec(memory_space=pltpu.SMEM)]
        + [pl.BlockSpec((rows, p.shape[1]), lambda i: (high, 0)) for p in payloads],
        out_specs=[pl.BlockSpec(shape, lambda i: (0, 0)) for shape in shapes],
        out_shape=[jax.ShapeDtypeStruct(shape, jnp.bfloat16) for shape in shapes],
        cost_estimate=pl.CostEstimate(flops=10**7, bytes_accessed=4 * shapes[0][0] * chunk, transcendentals=0),
        name="choose",
        interpret=INTERPRET,
    )(at_x, *payloads)


def project_kernel(count, *refs):
    context = jnp.concatenate([r[...] for r in refs[:count]], axis=1)
    weight = jnp.concatenate([r[...] for r in refs[count : 2 * count]], axis=0)
    refs[-1][...] = jnp.dot(context, weight, preferred_element_type=jnp.float32).astype(jnp.bfloat16)


def project(contexts, payloads, chunk):
    rows, width = contexts[0].shape
    part = min(256, rows)
    count = len(contexts)
    return pl.pallas_call(
        functools.partial(project_kernel, count),
        grid=(rows // part,),
        in_specs=[pl.BlockSpec((part, width), lambda i: (i, 0))] * count
        + [pl.BlockSpec((width, chunk), lambda i: (0, 0))] * count,
        out_specs=pl.BlockSpec((part, chunk), lambda i: (i, 0)),
        out_shape=jax.ShapeDtypeStruct((rows, chunk), jnp.bfloat16),
        cost_estimate=pl.CostEstimate(
            flops=2 * rows * width * count * chunk,
            bytes_accessed=2 * (rows * width * count + width * count * chunk + rows * chunk),
            transcendentals=0,
        ),
        name="project",
        interpret=INTERPRET,
    )(*contexts, *payloads)


def norm_kernel(groups, chunks, in_ref, gain_ref, out_ref):
    rows, chunk = in_ref.shape[1:]
    for group in range(groups):
        parts = [in_ref[group * chunks + i].astype(jnp.float32) for i in range(chunks)]
        squares = sum(jnp.sum(p * p, axis=1, keepdims=True) for p in parts)
        scale = lax.rsqrt(squares * (1.0 / (chunks * chunk)) + 1e-06)
        for i, p in enumerate(parts):
            gain = gain_ref[:, i * chunk : (i + 1) * chunk]
            out_ref[group * rows : (group + 1) * rows, i * chunk : (i + 1) * chunk] = (
                p * scale * gain
            ).astype(jnp.bfloat16)


def norm_rows(incoming, gain, groups, chunks):
    rows, chunk = incoming.shape[1:]
    shape = (groups * rows, chunks * chunk)
    return pl.pallas_call(
        functools.partial(norm_kernel, groups, chunks),
        in_specs=[pl.BlockSpec(memory_space=pltpu.VMEM)] * 2,
        out_shape=jax.ShapeDtypeStruct(shape, jnp.bfloat16),
        cost_estimate=pl.CostEstimate(
            flops=4 * shape[0] * shape[1], bytes_accessed=4 * shape[0] * shape[1], transcendentals=shape[0]
        ),
        name="norm_rows",
        interpret=INTERPRET,
    )(in_vmem(incoming), gain[None, :])


def expert_block(own, other, gate_up, down_weight):
    slice_width = down_weight.shape[0]
    half = own.shape[0]
    rows = jnp.concatenate([own, other], axis=0)
    gate_and_up = jnp.dot(rows, gate_up, preferred_element_type=jnp.float32)
    hidden = (jax.nn.silu(gate_and_up[:, :slice_width]) * gate_and_up[:, slice_width:]).astype(
        jnp.bfloat16
    )
    out_other = jnp.dot(hidden[half:], down_weight, preferred_element_type=jnp.float32)
    out_other = out_other.astype(jnp.bfloat16)
    out_own = jnp.dot(hidden[:half], down_weight, preferred_element_type=jnp.float32)
    return add_rounded(out_own, swap(out_other))


def add_rounded(a, b):
    return (a.astype(jnp.float32) + b.astype(jnp.float32)).astype(jnp.bfloat16)


def last_sum_kernel(own_ref, low_a, low_b, high_a, high_b, out_ref):
    half = low_a.shape[0]
    wide = own_ref.shape[1] // 2
    for start, first, second in ((0, low_a, low_b), (half, high_a, high_b)):
        for at in range(0, half, CAP):
            rows = slice(start + at, start + at + CAP)
            whole = (
                own_ref[rows].astype(jnp.float32)
                + first[at : at + CAP].astype(jnp.float32)
                + second[at : at + CAP].astype(jnp.float32)
            )
            both = jnp.concatenate([whole[:, :wide], whole[:, wide:]], axis=0)
            out_ref[(start + at) // CAP] = both.astype(jnp.bfloat16)


def last_sum(own, low_a, low_b, high_a, high_b):
    rows, width = own.shape
    shape = (rows // CAP, 2 * CAP, width // 2)
    return pl.pallas_call(
        last_sum_kernel,
        out_shape=jax.ShapeDtypeStruct(shape, jnp.bfloat16),
        cost_estimate=pl.CostEstimate(
            flops=2 * rows * width, bytes_accessed=8 * rows * width, transcendentals=0
        ),
        name="last_sum",
        interpret=INTERPRET,
    )(own, low_a, low_b, high_a, high_b)


def combine_kernel(picked_ref, returned_ref, out_ref):
    rows, wide = out_ref.shape[0], returned_ref.shape[1]
    both = jnp.dot(picked_ref[...], returned_ref[...], preferred_element_type=jnp.float32)
    for half in range(2):
        out_ref[:, half * wide : (half + 1) * wide] = both[half * rows : (half + 1) * rows].astype(
            jnp.bfloat16
        )


def combine(picked, returned):
    shape = (picked.shape[0] // 2, 2 * returned.shape[1])
    return pl.pallas_call(
        combine_kernel,
        in_specs=[pl.BlockSpec(memory_space=pltpu.VMEM)] * 2,
        out_shape=jax.ShapeDtypeStruct(shape, jnp.bfloat16),
        cost_estimate=pl.CostEstimate(
            flops=2 * picked.shape[0] * returned.size,
            bytes_accessed=2 * (returned.size + shape[0] * shape[1]),
            transcendentals=0,
        ),
        name="combine",
        interpret=INTERPRET,
    )(picked, in_vmem(returned))


def on_device(
    queries, doc_keys, doc_values, residual, out_weight, norm_gain, expert_ids, gate_up, down_weight
):
    nx, nzlo, ny, nzhi = (lax.axis_size(a) for a in ("x", "zlo", "y", "zhi"))
    rows, width = residual.shape
    chunk = width // nx
    group = nzlo * ny
    experts = nx * nzlo

    at_x = lax.axis_index("x").astype(jnp.int32).reshape(1)
    ordered = queries.reshape(nx, group, rows, -1).transpose(1, 0, 2, 3).reshape(queries.shape)
    sent = pack(at_x, residual, expert_ids, out_weight)
    payloads = [sent[0]] + [shift(p, "x", step) for p, step in zip(sent[1:], X_STEPS[1:])]
    residual_chunk, chosen = choose(at_x, payloads, rows, chunk, nx, nzlo)
    context, (payloads, residual_chunk, chosen) = attention(
        ordered, doc_keys, doc_values, (payloads, residual_chunk, chosen)
    )
    contexts = [context] + [shift(context, "x", step) for step in X_STEPS[1:]]
    partial_rows = project(contexts, payloads, chunk)
    pieces = lax.all_to_all(
        partial_rows.reshape(group, nx * rows, chunk), ("zlo", "y"), split_axis=0, concat_axis=0, tiled=True
    )
    mixed = jnp.sum(pieces.astype(jnp.float32), axis=0)
    attended_chunk = (residual_chunk.astype(jnp.float32) + mixed).astype(jnp.bfloat16)
    attended = lax.all_to_all(attended_chunk, "x", split_axis=0, concat_axis=1, tiled=True)

    outgoing = jnp.dot(chosen, attended_chunk, preferred_element_type=jnp.float32).astype(jnp.bfloat16)
    outgoing = outgoing.reshape(1, experts, nx * CAP, chunk)
    outgoing = jnp.broadcast_to(outgoing, (nzhi,) + outgoing.shape[1:]).reshape(
        nzhi * experts, nx * CAP, chunk
    )
    incoming = lax.all_to_all(outgoing, PLANE, split_axis=0, concat_axis=0, tiled=True)
    normed = norm_rows(incoming, norm_gain, nzhi * nzlo, nx)

    half = normed.shape[0] // 2
    gate_up, down_weight = gate_up[0], down_weight[0]
    from_prev, from_next = shift(normed, "y", 1), shift(normed, "y", -1)
    sum_own = expert_block(normed, swap(normed), gate_up, down_weight)
    far_a = shift(from_prev[:half], "y", 1)
    far_b = shift(from_next[half:], "y", -1)
    sum_prev = expert_block(from_prev, swap(from_prev), gate_up, down_weight)
    sum_next = expert_block(from_next, swap(from_next), gate_up, down_weight)
    early_next = shift(sum_next[half:], "y", 1)
    early_prev = shift(sum_prev[:half], "y", -1)
    far = jnp.concatenate([far_a, far_b], axis=0)
    sum_far = expert_block(far, swap(far), gate_up, down_weight)
    relay_next, relay_prev = shift(sum_far[:half], "y", 1), shift(sum_far[half:], "y", -1)
    late_next = shift(add_rounded(sum_next[:half], relay_next), "y", 1)
    late_prev = shift(add_rounded(sum_prev[half:], relay_prev), "y", -1)
    summed = last_sum(sum_own, late_next, early_prev, early_next, late_prev)
    returned = lax.all_to_all(summed, PLANE, split_axis=0, concat_axis=0, tiled=True)
    own_routes = expert_ids[:, 0]
    positions = jnp.arange(rows, dtype=jnp.int32)
    slots = jnp.arange(CAP, dtype=jnp.int32)
    expert_of = (
        jnp.arange(nx, dtype=jnp.int32)[None, :] * nzlo + jnp.arange(nzlo, dtype=jnp.int32)[:, None]
    ).reshape(-1)
    own_earlier = (own_routes[:, None] == own_routes[None, :]) & (positions[:, None] > positions[None, :])
    own_rank = jnp.sum(own_earlier.astype(jnp.int32), axis=1)
    picked = (own_routes[:, None, None] == expert_of[None, :, None]) & (
        own_rank[:, None, None] == slots[None, None, :]
    )
    halves = jnp.arange(2, dtype=jnp.int32)
    picked = (halves[:, None] == halves[None, :])[:, None, None, None, :, None] & jnp.broadcast_to(
        picked[None, :, None, :, None, :], (1, rows, nzhi, nx * nzlo, 1, CAP)
    )
    expert_sum = combine(
        picked.reshape(2 * rows, -1).astype(jnp.bfloat16), returned.reshape(-1, width // 2)
    )
    return (attended, expert_sum)


def solution(mesh):
    split = Mesh(mesh.devices.reshape(4, 2, 4, 2, 4), CTX + EXP)
    return jax.shard_map(
        on_device,
        mesh=split,
        in_specs=(
            P(CTX, EXP),
            P(CTX, EXP),
            P(CTX, EXP),
            P(CTX + EXP, None),
            P(EXP, None),
            P(),
            P(CTX + EXP, None),
            P(EXP, None, CTX),
            P(EXP, CTX, None),
        ),
        out_specs=(P(CTX + EXP, None), P(CTX + EXP, None)),
        check_vma=False,
    )
```

```python
import functools

import jax
import jax.numpy as jnp
from jax import lax
from jax.experimental import pallas as pl
from jax.experimental.pallas import tpu as pltpu
from jax.sharding import Mesh
from jax.sharding import PartitionSpec as P

DH = 64
CAP = 4
CTX = ("zhi", "core")
EXP = ("x", "zlo", "y")
PLANE = ("zhi", "zlo", "x")
INTERPRET = False


SPLIT = 2
X_STEPS = (0, 1, -1, 2)


def shift(value, axis, step):
    size = lax.axis_size(axis)
    return lax.ppermute(value, axis, [(i, (i + step) % size) for i in range(size)])


def swap(value):
    return shift(value, "core", 1)


def in_vmem(value):
    return value if INTERPRET else pltpu.with_memory_space_constraint(value, pltpu.VMEM)


def attend_kernel(count, first, last, *refs):
    q_ref, keys, values = refs[0], refs[1 : 1 + count], refs[1 + count : 1 + 2 * count]
    rest = refs[1 + 2 * count :]
    if not first:
        acc_in, top_in, total_in = rest[:3]
        rest = rest[3:]
    head = pl.program_id(1)
    queries = q_ref[...]
    mine = lax.broadcasted_iota(jnp.int32, queries.shape, 1) // DH == head
    own = jnp.where(mine, queries, jnp.zeros_like(queries)) * jnp.asarray(DH**-0.5, queries.dtype)
    if first:
        top = jnp.full((queries.shape[0], 1), -jnp.inf, jnp.float32)
        total = jnp.zeros((queries.shape[0], 1), jnp.float32)
        acc = jnp.zeros(queries.shape, jnp.float32)
    else:
        top = jnp.max(jnp.where(mine, top_in[...], -jnp.inf), axis=1, keepdims=True)
        total = jnp.max(jnp.where(mine, total_in[...], 0.0), axis=1, keepdims=True)
        acc = acc_in[...]
    for key, value in zip(keys, values):
        scores = lax.dot_general(
            own, key[...], (((1,), (1,)), ((), ())), preferred_element_type=jnp.float32
        )
        new_top = jnp.maximum(top, jnp.max(scores, axis=1, keepdims=True))
        decay = jnp.exp(top - new_top)
        weights = jnp.exp(scores - new_top)
        total = total * decay + jnp.sum(weights, axis=1, keepdims=True)
        acc = acc * decay + jnp.dot(
            weights.astype(jnp.bfloat16), value[...], preferred_element_type=jnp.float32
        )
        top = new_top
    if last:
        results = ((acc / total).astype(jnp.bfloat16),)
    else:
        results = (acc, jnp.broadcast_to(top, acc.shape), jnp.broadcast_to(total, acc.shape))

    @pl.when(head == 0)
    def _():
        for ref, result in zip(rest, results):
            ref[...] = result

    @pl.when(head != 0)
    def _():
        for ref, result in zip(rest, results):
            ref[...] = jnp.where(mine, result, ref[...])


def attend(queries, keys, values, state, last):
    total_rows, width = queries.shape
    rows = min(256, total_rows)
    heads = width // DH
    whole = [pl.BlockSpec(k.shape, lambda i, h: (0, 0)) for k in keys + values]
    part = pl.BlockSpec((rows, width), lambda i, h: (i, 0))
    docs = sum(k.shape[0] for k in keys)
    if last:
        shapes = [jax.ShapeDtypeStruct(queries.shape, jnp.bfloat16)]
    else:
        shapes = [jax.ShapeDtypeStruct(queries.shape, jnp.float32)] * 3
    return pl.pallas_call(
        functools.partial(attend_kernel, len(keys), not state, last),
        grid=(total_rows // rows, heads),
        in_specs=[part] + whole + [part] * len(state),
        out_specs=[part] * len(shapes),
        out_shape=shapes,
        cost_estimate=pl.CostEstimate(
            flops=4 * total_rows * docs * width,
            bytes_accessed=4 * docs * width + 14 * total_rows * width,
            transcendentals=heads * total_rows * docs,
        ),
        interpret=INTERPRET,
    )(queries, *keys, *values, *state)


def attention(queries, keys, values, early):
    near_keys = [swap(keys), shift(keys, "zhi", 1), shift(keys, "zhi", -1)]
    near_values = [swap(values), shift(values, "zhi", 1), shift(values, "zhi", -1)]
    state = attend(queries, [keys, near_keys[0]], [values, near_values[0]], [], False)
    far_key = shift(near_keys[1], "zhi", 1)
    far_value = shift(near_values[2], "zhi", -1)
    state = attend(
        queries,
        near_keys[1:] + [swap(k) for k in near_keys[1:]],
        near_values[1:] + [swap(v) for v in near_values[1:]],
        state,
        False,
    )
    state, far_key, far_value, early = lax.optimization_barrier((state, far_key, far_value, early))
    (context,) = attend(queries, [far_key, swap(far_key)], [far_value, swap(far_value)], state, True)
    return context, early


def pack_kernel(x_ref, residual_ref, ids_ref, weight_ref, *out_refs):
    wide, chunk = weight_ref.shape[0], weight_ref.shape[1] // len(out_refs)
    rows = residual_ref.shape[0]
    row = lax.broadcasted_iota(jnp.int32, (rows, rows), 0)
    column = lax.broadcasted_iota(jnp.int32, (rows, rows), 1)
    ids = jnp.where(row == column, jnp.broadcast_to(ids_ref[...], (rows, rows)).astype(jnp.float32), 0.0)
    ids = jnp.sum(ids, axis=1, keepdims=True)
    for step, out_ref in zip(X_STEPS, out_refs):
        at = pl.multiple_of((x_ref[0] + step + 4) % 4 * chunk, chunk)
        out_ref[:wide, :chunk] = weight_ref[:, pl.ds(at, chunk)]
        out_ref[:wide, chunk:] = jnp.zeros((wide, out_ref.shape[1] - chunk), jnp.bfloat16)
        out_ref[wide:, :chunk] = residual_ref[:, pl.ds(at, chunk)]
        out_ref[wide:, chunk:] = jnp.broadcast_to(ids, (rows, out_ref.shape[1] - chunk)).astype(jnp.bfloat16)


def pack(at_x, residual, ids, weight):
    nx = lax.axis_size("x")
    shape = (weight.shape[0] + residual.shape[0], weight.shape[1] // nx + 128)
    vmem = pl.BlockSpec(memory_space=pltpu.VMEM)
    return pl.pallas_call(
        pack_kernel,
        in_specs=[pl.BlockSpec(memory_space=pltpu.SMEM), vmem, vmem, vmem],
        out_shape=[jax.ShapeDtypeStruct(shape, jnp.bfloat16)] * nx,
        cost_estimate=pl.CostEstimate(
            flops=0, bytes_accessed=4 * weight.shape[0] * weight.shape[1], transcendentals=0
        ),
        name="pack",
        interpret=INTERPRET,
    )(at_x, residual, ids, weight)


def choose_kernel(nx, nzlo, x_ref, *refs):
    parts, (residual_ref, chosen_ref) = refs[:nx], refs[nx:]
    rows, chunk = parts[0].shape[0], residual_ref.shape[1]
    tokens = nx * rows
    got = jnp.concatenate([p[...].astype(jnp.float32) for p in parts], axis=0)
    row = lax.broadcasted_iota(jnp.int32, (tokens, tokens), 0)
    column = lax.broadcasted_iota(jnp.int32, (tokens, tokens), 1)
    source = jnp.zeros((tokens, tokens), jnp.int32)
    for at, step in enumerate(X_STEPS):
        source = jnp.where(row // rows == (x_ref[0] - step + 4) % 4, at * rows + row % rows, source)
    order = (column == source).astype(jnp.bfloat16)
    ordered = jnp.dot(order, got.astype(jnp.bfloat16), preferred_element_type=jnp.float32)
    residual_ref[...] = ordered[:, :chunk].astype(jnp.bfloat16)
    by_row = ordered[:, chunk : chunk + tokens]
    by_column = jnp.sum(jnp.where(row == column, by_row, 0.0), axis=0, keepdims=True)
    earlier = (by_row == by_column) & (row // rows == column // rows) & (row < column)
    rank = jnp.sum(earlier.astype(jnp.float32), axis=0, keepdims=True)
    slots = chosen_ref.shape[0]
    row = lax.broadcasted_iota(jnp.int32, (slots, tokens), 0)
    column = lax.broadcasted_iota(jnp.int32, (slots, tokens), 1)
    low = CAP // SPLIT
    part_rows = slots // SPLIT
    plane = row % part_rows // (nx * low)
    expert = (plane % nx * nzlo + plane // nx).astype(jnp.float32)
    chosen = (
        (by_column == expert)
        & (rank == (row // part_rows * low + row % low).astype(jnp.float32))
        & (row // low % nx == column // rows)
    )
    chosen_ref[...] = chosen.astype(jnp.bfloat16)


def choose(at_x, payloads, rows, chunk, nx, nzlo):
    high = payloads[0].shape[0] // rows - 1
    shapes = [(nx * rows, chunk), (nx * nzlo * nx * CAP, nx * rows)]
    return pl.pallas_call(
        functools.partial(choose_kernel, nx, nzlo),
        grid=(1,),
        in_specs=[pl.BlockSpec(memory_space=pltpu.SMEM)]
        + [pl.BlockSpec((rows, p.shape[1]), lambda i: (high, 0)) for p in payloads],
        out_specs=[pl.BlockSpec(shape, lambda i: (0, 0)) for shape in shapes],
        out_shape=[jax.ShapeDtypeStruct(shape, jnp.bfloat16) for shape in shapes],
        cost_estimate=pl.CostEstimate(flops=10**7, bytes_accessed=4 * shapes[0][0] * chunk, transcendentals=0),
        name="choose",
        interpret=INTERPRET,
    )(at_x, *payloads)


def project_kernel(count, *refs):
    context = jnp.concatenate([r[...] for r in refs[:count]], axis=1)
    weight = jnp.concatenate([r[...] for r in refs[count : 2 * count]], axis=0)
    out = jnp.dot(context, weight, preferred_element_type=jnp.float32).astype(jnp.bfloat16)
    out_ref = refs[-1]
    groups, rows = out_ref.shape[0], out_ref.shape[2]
    for group in range(groups):
        out_ref[group, 0] = out[group * rows : (group + 1) * rows]


def project(contexts, payloads, chunk, groups):
    rows, width = contexts[0].shape
    count = len(contexts)
    part = rows // count
    shape = (groups, count, part // groups, chunk)
    return pl.pallas_call(
        functools.partial(project_kernel, count),
        grid=(count,),
        in_specs=[pl.BlockSpec((part, width), lambda i: (i, 0))] * count
        + [pl.BlockSpec((width, chunk), lambda i: (0, 0))] * count,
        out_specs=pl.BlockSpec((groups, 1, part // groups, chunk), lambda i: (0, i, 0, 0)),
        out_shape=jax.ShapeDtypeStruct(shape, jnp.bfloat16),
        cost_estimate=pl.CostEstimate(
            flops=2 * rows * width * count * chunk,
            bytes_accessed=2 * (rows * width * count + width * count * chunk + rows * chunk),
            transcendentals=0,
        ),
        name="project",
        interpret=INTERPRET,
    )(*contexts, *payloads)


def norm_kernel(groups, chunks, in_ref, gain_ref, out_ref):
    rows, chunk = in_ref.shape[1:]
    for group in range(0, groups, 2):
        parts = [
            jnp.concatenate(
                [in_ref[(group + j) * chunks + i].astype(jnp.float32) for j in range(2)], axis=0
            )
            for i in range(chunks)
        ]
        squares = sum(jnp.sum(p * p, axis=1, keepdims=True) for p in parts)
        scale = lax.rsqrt(squares * (1.0 / (chunks * chunk)) + 1e-06)
        for i, p in enumerate(parts):
            gain = gain_ref[:, i * chunk : (i + 1) * chunk]
            out_ref[group * rows : (group + 2) * rows, i * chunk : (i + 1) * chunk] = (
                p * scale * gain
            ).astype(jnp.bfloat16)


def norm_rows(incoming, gain, groups, chunks):
    rows, chunk = incoming.shape[1:]
    shape = (groups * rows, chunks * chunk)
    return pl.pallas_call(
        functools.partial(norm_kernel, groups, chunks),
        in_specs=[pl.BlockSpec(memory_space=pltpu.VMEM)] * 2,
        out_shape=jax.ShapeDtypeStruct(shape, jnp.bfloat16),
        cost_estimate=pl.CostEstimate(
            flops=4 * shape[0] * shape[1], bytes_accessed=4 * shape[0] * shape[1], transcendentals=shape[0]
        ),
        name="norm_rows",
        interpret=INTERPRET,
    )(in_vmem(incoming), gain[None, :])


def expert_block(own, other, gate_up, down_weight):
    slice_width = down_weight.shape[0]
    half = own.shape[0]
    rows = jnp.concatenate([own, other], axis=0)
    gate_and_up = jnp.dot(rows, gate_up, preferred_element_type=jnp.float32)
    hidden = (jax.nn.silu(gate_and_up[:, :slice_width]) * gate_and_up[:, slice_width:]).astype(
        jnp.bfloat16
    )
    out_other = jnp.dot(hidden[half:], down_weight, preferred_element_type=jnp.float32)
    out_other = out_other.astype(jnp.bfloat16)
    out_own = jnp.dot(hidden[:half], down_weight, preferred_element_type=jnp.float32)
    return add_rounded(out_own, swap(out_other))


def add_rounded(a, b):
    return (a.astype(jnp.float32) + b.astype(jnp.float32)).astype(jnp.bfloat16)


def last_sum_kernel(first_ref, second_ref, third_ref, out_ref):
    slots = CAP // SPLIT
    parts = out_ref.shape[1] // slots
    wide = out_ref.shape[2]
    slab = 16
    for at in range(0, first_ref.shape[0], slab):
        whole = sum(r[at : at + slab].astype(jnp.float32) for r in (first_ref, second_ref, third_ref))
        for row in range(0, slab, slots):
            pieces = [whole[row : row + slots, i * wide : (i + 1) * wide] for i in range(parts)]
            out_ref[(at + row) // slots] = jnp.concatenate(pieces, axis=0).astype(jnp.bfloat16)


def last_sum(first, second, third):
    rows, width = first.shape
    slots = CAP // SPLIT
    parts = 8 // slots
    shape = (rows // slots, parts * slots, width // parts)
    return pl.pallas_call(
        last_sum_kernel,
        out_shape=jax.ShapeDtypeStruct(shape, jnp.bfloat16),
        cost_estimate=pl.CostEstimate(
            flops=2 * rows * width, bytes_accessed=8 * rows * width, transcendentals=0
        ),
        name="last_sum",
        interpret=INTERPRET,
    )(first, second, third)


def combine_kernel(picked_a, picked_b, returned_a, returned_b, out_ref):
    rows, wide = out_ref.shape[0], returned_a.shape[1]
    both = jnp.dot(picked_a[...], returned_a[...], preferred_element_type=jnp.float32)
    both = both + jnp.dot(picked_b[...], returned_b[...], preferred_element_type=jnp.float32)
    for part in range(picked_a.shape[0] // rows):
        out_ref[:, part * wide : (part + 1) * wide] = both[part * rows : (part + 1) * rows].astype(
            jnp.bfloat16
        )


def combine(picked, returned, rows):
    parts = picked[0].shape[0] // rows
    shape = (rows, parts * returned[0].shape[1])
    return pl.pallas_call(
        combine_kernel,
        in_specs=[pl.BlockSpec(memory_space=pltpu.VMEM)] * 4,
        out_shape=jax.ShapeDtypeStruct(shape, jnp.bfloat16),
        cost_estimate=pl.CostEstimate(
            flops=4 * picked[0].shape[0] * returned[0].size,
            bytes_accessed=4 * returned[0].size + 2 * shape[0] * shape[1],
            transcendentals=0,
        ),
        name="combine",
        interpret=INTERPRET,
    )(*picked, *[in_vmem(r) for r in returned])


def on_device(
    queries, doc_keys, doc_values, residual, out_weight, norm_gain, expert_ids, gate_up, down_weight
):
    nx, nzlo, ny, nzhi = (lax.axis_size(a) for a in ("x", "zlo", "y", "zhi"))
    rows, width = residual.shape
    chunk = width // nx
    group = nzlo * ny
    experts = nx * nzlo

    at_x = lax.axis_index("x").astype(jnp.int32).reshape(1)
    sent = pack(at_x, residual, expert_ids.reshape(1, rows), out_weight)
    payloads = [sent[0]] + [shift(p, "x", step) for p, step in zip(sent[1:], X_STEPS[1:])]
    residual_chunk, chosen = choose(at_x, payloads, rows, chunk, nx, nzlo)
    context, (payloads, residual_chunk, chosen) = attention(
        queries, doc_keys, doc_values, (payloads, residual_chunk, chosen)
    )
    contexts = [context] + [shift(context, "x", step) for step in X_STEPS[1:]]
    partial_rows = project(contexts, payloads, chunk, group)
    pieces = lax.all_to_all(
        partial_rows.reshape(group, nx * rows, chunk), ("zlo", "y"), split_axis=0, concat_axis=0, tiled=True
    )
    mixed = jnp.sum(pieces.astype(jnp.float32), axis=0)
    attended_chunk = (residual_chunk.astype(jnp.float32) + mixed).astype(jnp.bfloat16)

    half = chosen.shape[0] // SPLIT

    def dispatch(part):
        outgoing = jnp.dot(
            chosen[part * half : (part + 1) * half], attended_chunk, preferred_element_type=jnp.float32
        ).astype(jnp.bfloat16)
        outgoing = outgoing.reshape(1, experts, half // experts, chunk)
        outgoing = jnp.broadcast_to(outgoing, (nzhi,) + outgoing.shape[1:])
        outgoing = outgoing.reshape(nzhi * experts, half // experts, chunk)
        incoming = lax.all_to_all(outgoing, PLANE, split_axis=0, concat_axis=0, tiled=True)
        return norm_rows(incoming, norm_gain, nzhi * nzlo, nx)

    gate_up, down_weight = gate_up[0], down_weight[0]
    rows_a = dispatch(0)
    prev_a, next_a = shift(rows_a, "y", 1), shift(rows_a, "y", -1)
    other_a = swap(rows_a)
    attended_chunk, rows_a = lax.optimization_barrier((attended_chunk, rows_a))
    rows_b = dispatch(1)
    prev_b, next_b = shift(rows_b, "y", 1), shift(rows_b, "y", -1)
    other_b = swap(rows_b)
    far_a, far_b = shift(prev_a, "y", 1), shift(next_b, "y", -1)

    def block(own, other):
        return expert_block(own, other, gate_up, down_weight)

    own_sum_a = block(rows_a, other_a)
    prev_sum_a = block(prev_a, swap(prev_a))
    next_sum_a = block(next_a, swap(next_a))
    early_a = shift(prev_sum_a, "y", -1)
    far_sum_a = block(far_a, swap(far_a))
    relay_a = shift(far_sum_a, "y", 1)
    own_sum_b = block(rows_b, other_b)
    prev_sum_b = block(prev_b, swap(prev_b))
    next_sum_b = block(next_b, swap(next_b))
    early_b = shift(next_sum_b, "y", 1)
    far_sum_b = block(far_b, swap(far_b))
    relay_b = shift(far_sum_b, "y", -1)
    finished, _ = lax.optimization_barrier((attended_chunk, far_sum_b))
    attended = lax.all_to_all(finished, "x", split_axis=0, concat_axis=1, tiled=True)
    late_a = shift(add_rounded(next_sum_a, relay_a), "y", 1)
    late_b = shift(add_rounded(prev_sum_b, relay_b), "y", -1)
    returned = []
    for pieces in ((own_sum_a, early_a, late_a), (own_sum_b, early_b, late_b)):
        summed = last_sum(*pieces)
        returned.append(lax.all_to_all(summed, PLANE, split_axis=0, concat_axis=0, tiled=True))
    own_routes = expert_ids[:, 0]
    positions = jnp.arange(rows, dtype=jnp.int32)
    slots = jnp.arange(CAP, dtype=jnp.int32)
    expert_of = (
        jnp.arange(nx, dtype=jnp.int32)[None, :] * nzlo + jnp.arange(nzlo, dtype=jnp.int32)[:, None]
    ).reshape(-1)
    own_earlier = (own_routes[:, None] == own_routes[None, :]) & (positions[:, None] > positions[None, :])
    own_rank = jnp.sum(own_earlier.astype(jnp.int32), axis=1)
    low = CAP // SPLIT
    parts = returned[0].shape[1] // low
    same = jnp.arange(parts, dtype=jnp.int32)
    same = (same[:, None] == same[None, :])[:, None, None, None, :, None]
    named = (own_routes[:, None] == expert_of[None, :])[None, :, None, :, None, None]
    picked = []
    for part in range(SPLIT):
        ranked = (own_rank[:, None] == slots[None, part * low : (part + 1) * low])[
            None, :, None, None, None, :
        ]
        chosen_rows = jnp.broadcast_to(same & named & ranked, (parts, rows, nzhi, nx * nzlo, parts, low))
        picked.append(chosen_rows.reshape(parts * rows, -1).astype(jnp.bfloat16))
    expert_sum = combine(picked, [r.reshape(-1, r.shape[2]) for r in returned], rows)
    return (attended, expert_sum)


def solution(mesh):
    split = Mesh(mesh.devices.reshape(4, 2, 4, 2, 4), CTX + EXP)
    return jax.shard_map(
        on_device,
        mesh=split,
        in_specs=(
            P(CTX, EXP),
            P(CTX, EXP),
            P(CTX, EXP),
            P(CTX + EXP, None),
            P(EXP, None),
            P(),
            P(CTX + EXP, None),
            P(EXP, None, CTX),
            P(EXP, CTX, None),
        ),
        out_specs=(P(CTX + EXP, None), P(CTX + EXP, None)),
        check_vma=False,
    )
```

```python
import functools

import jax
import jax.numpy as jnp
from jax import lax
from jax.experimental import pallas as pl
from jax.experimental.pallas import tpu as pltpu
from jax.sharding import Mesh
from jax.sharding import PartitionSpec as P

DH = 64
CAP = 4
CTX = ("zhi", "core")
EXP = ("x", "zlo", "y")
PLANE = ("zhi", "zlo", "x")
INTERPRET = False


X_STEPS = (0, 1, -1, 2)
DEEP = 512


def shift(value, axis, step):
    size = lax.axis_size(axis)
    return lax.ppermute(value, axis, [(i, (i + step) % size) for i in range(size)])


def swap(value):
    return shift(value, "core", 1)


def in_vmem(value):
    return value if INTERPRET else pltpu.with_memory_space_constraint(value, pltpu.VMEM)


def attend_kernel(count, first, last, *refs):
    q_ref, keys, values = refs[0], refs[1 : 1 + count], refs[1 + count : 1 + 2 * count]
    rest = refs[1 + 2 * count :]
    if not first:
        acc_in, top_in, total_in = rest[:3]
        rest = rest[3:]
    head = pl.program_id(1)
    queries = q_ref[...]
    mine = lax.broadcasted_iota(jnp.int32, queries.shape, 1) // DH == head
    own = jnp.where(mine, queries, jnp.zeros_like(queries)) * jnp.asarray(DH**-0.5, queries.dtype)
    if first:
        top = jnp.full((queries.shape[0], 1), -jnp.inf, jnp.float32)
        total = jnp.zeros((queries.shape[0], 1), jnp.float32)
        acc = jnp.zeros(queries.shape, jnp.float32)
    else:
        top = jnp.max(jnp.where(mine, top_in[...], -jnp.inf), axis=1, keepdims=True)
        total = jnp.max(jnp.where(mine, total_in[...], 0.0), axis=1, keepdims=True)
        acc = acc_in[...]
    for key, value in zip(keys, values):
        scores = lax.dot_general(
            own, key[...], (((1,), (1,)), ((), ())), preferred_element_type=jnp.float32
        )
        new_top = jnp.maximum(top, jnp.max(scores, axis=1, keepdims=True))
        decay = jnp.exp(top - new_top)
        weights = jnp.exp(scores - new_top)
        total = total * decay + jnp.sum(weights, axis=1, keepdims=True)
        acc = acc * decay + jnp.dot(
            weights.astype(jnp.bfloat16), value[...], preferred_element_type=jnp.float32
        )
        top = new_top
    if last:
        results = ((acc / total).astype(jnp.bfloat16),)
    else:
        results = (acc, jnp.broadcast_to(top, acc.shape), jnp.broadcast_to(total, acc.shape))

    @pl.when(head == 0)
    def _():
        for ref, result in zip(rest, results):
            ref[...] = result

    @pl.when(head != 0)
    def _():
        for ref, result in zip(rest, results):
            ref[...] = jnp.where(mine, result, ref[...])


def attend(queries, keys, values, state, last):
    total_rows, width = queries.shape
    rows = min(128, total_rows)
    heads = width // DH
    whole = [pl.BlockSpec(k.shape, lambda i, h: (0, 0)) for k in keys + values]
    part = pl.BlockSpec((rows, width), lambda i, h: (i, 0))
    docs = sum(k.shape[0] for k in keys)
    if last:
        shapes = [jax.ShapeDtypeStruct(queries.shape, jnp.bfloat16)]
    else:
        shapes = [jax.ShapeDtypeStruct(queries.shape, jnp.float32)] * 3
    return pl.pallas_call(
        functools.partial(attend_kernel, len(keys), not state, last),
        grid=(total_rows // rows, heads),
        in_specs=[part] + whole + [part] * len(state),
        out_specs=[part] * len(shapes),
        out_shape=shapes,
        cost_estimate=pl.CostEstimate(
            flops=4 * total_rows * docs * width,
            bytes_accessed=4 * docs * width + 14 * total_rows * width,
            transcendentals=heads * total_rows * docs,
        ),
        interpret=INTERPRET,
    )(queries, *keys, *values, *state)


def attention(queries, keys, values, early):
    near_keys = [swap(keys), shift(keys, "zhi", 1), shift(keys, "zhi", -1)]
    near_values = [swap(values), shift(values, "zhi", 1), shift(values, "zhi", -1)]
    state = attend(queries, [keys, near_keys[0]], [values, near_values[0]], [], False)
    far_key = shift(near_keys[1], "zhi", 1)
    far_value = shift(near_values[2], "zhi", -1)
    state = attend(
        queries,
        near_keys[1:] + [swap(k) for k in near_keys[1:]],
        near_values[1:] + [swap(v) for v in near_values[1:]],
        state,
        False,
    )
    state, far_key, far_value, early = lax.optimization_barrier((state, far_key, far_value, early))
    (context,) = attend(queries, [far_key, swap(far_key)], [far_value, swap(far_value)], state, True)
    return context, early


def pack_kernel(residual_ref, ids_ref, weight_ref, out_ref):
    wide, chunk = weight_ref.shape[0], weight_ref.shape[1] // out_ref.shape[0]
    rest = out_ref.shape[2] - chunk
    rows = residual_ref.shape[0]
    ids = jnp.broadcast_to(ids_ref[...].astype(jnp.float32), (rows, rest)).astype(jnp.bfloat16)
    for part in range(out_ref.shape[0]):
        at = slice(part * chunk, (part + 1) * chunk)
        out_ref[part, :wide, :chunk] = weight_ref[:, at]
        out_ref[part, :wide, chunk:] = jnp.zeros((wide, rest), jnp.bfloat16)
        out_ref[part, wide:, :chunk] = residual_ref[:, at]
        out_ref[part, wide:, chunk:] = ids


def pack(residual, ids, weight):
    nx = lax.axis_size("x")
    shape = (nx, weight.shape[0] + residual.shape[0], weight.shape[1] // nx + 128)
    return pl.pallas_call(
        pack_kernel,
        in_specs=[pl.BlockSpec(memory_space=pltpu.VMEM)] * 3,
        out_shape=jax.ShapeDtypeStruct(shape, jnp.bfloat16),
        cost_estimate=pl.CostEstimate(
            flops=0, bytes_accessed=4 * weight.shape[0] * weight.shape[1], transcendentals=0
        ),
        name="pack",
        interpret=INTERPRET,
    )(residual, ids, weight)


def choose_kernel(nx, nzlo, got_ref, residual_ref, chosen_ref):
    rows, chunk = got_ref.shape[1], residual_ref.shape[1]
    tokens = nx * rows
    for part in range(nx):
        residual_ref[part * rows : (part + 1) * rows] = got_ref[part, :, :chunk]
    ids = [got_ref[part, :, chunk : chunk + tokens].astype(jnp.float32) for part in range(nx)]
    by_row = jnp.concatenate(ids, axis=0)
    row = lax.broadcasted_iota(jnp.int32, (tokens, tokens), 0)
    column = lax.broadcasted_iota(jnp.int32, (tokens, tokens), 1)
    by_column = jnp.sum(jnp.where(row == column, by_row, 0.0), axis=0, keepdims=True)
    earlier = (by_row == by_column) & (row // rows == column // rows) & (row < column)
    rank = jnp.sum(earlier.astype(jnp.float32), axis=0, keepdims=True)
    slots = chosen_ref.shape[0]
    row = lax.broadcasted_iota(jnp.int32, (slots, tokens), 0)
    column = lax.broadcasted_iota(jnp.int32, (slots, tokens), 1)
    plane = row // (nx * CAP)
    expert = (plane % nx * nzlo + plane // nx).astype(jnp.float32)
    chosen = (
        (by_column == expert)
        & (rank == (row % CAP).astype(jnp.float32))
        & (row // CAP % nx == column // rows)
    )
    chosen_ref[...] = chosen.astype(jnp.bfloat16)


def choose(payload, rows, chunk, nx, nzlo):
    high = payload.shape[1] // rows - 1
    shapes = [(nx * rows, chunk), (nx * nzlo * nx * CAP, nx * rows)]
    return pl.pallas_call(
        functools.partial(choose_kernel, nx, nzlo),
        grid=(1,),
        in_specs=[pl.BlockSpec((nx, rows, payload.shape[2]), lambda i: (0, high, 0))],
        out_specs=[pl.BlockSpec(shape, lambda i: (0, 0)) for shape in shapes],
        out_shape=[jax.ShapeDtypeStruct(shape, jnp.bfloat16) for shape in shapes],
        cost_estimate=pl.CostEstimate(flops=10**7, bytes_accessed=4 * shapes[0][0] * chunk, transcendentals=0),
        name="choose",
        interpret=INTERPRET,
    )(payload)


def project_kernel(chunk, x_ref, payload_ref, *refs):
    contexts, out_ref = refs[:-1], refs[-1]
    nx, width = len(contexts), contexts[0].shape[1]
    context = jnp.concatenate([r[...] for r in contexts], axis=1)
    weights = [payload_ref[(x_ref[0] - step + nx) % nx, :width, :chunk] for step in X_STEPS]
    weight = jnp.concatenate(weights, axis=0)
    out_ref[...] = jnp.dot(context, weight, preferred_element_type=jnp.float32).astype(jnp.bfloat16)


def project(at_x, contexts, payload, chunk):
    rows, width = contexts[0].shape
    part = min(256, rows)
    count = len(contexts)
    return pl.pallas_call(
        functools.partial(project_kernel, chunk),
        grid=(rows // part,),
        in_specs=[pl.BlockSpec(memory_space=pltpu.SMEM), pl.BlockSpec(payload.shape, lambda i: (0, 0, 0))]
        + [pl.BlockSpec((part, width), lambda i: (i, 0))] * count,
        out_specs=pl.BlockSpec((part, chunk), lambda i: (i, 0)),
        out_shape=jax.ShapeDtypeStruct((rows, chunk), jnp.bfloat16),
        cost_estimate=pl.CostEstimate(
            flops=2 * rows * width * count * chunk,
            bytes_accessed=2 * (rows * width * count + width * count * chunk + rows * chunk),
            transcendentals=0,
        ),
        name="project",
        interpret=INTERPRET,
    )(at_x, payload, *contexts)


def norm_kernel(groups, chunks, in_ref, gain_ref, out_ref):
    rows, chunk = in_ref.shape[1:]
    for group in range(groups):
        parts = [in_ref[group * chunks + i].astype(jnp.float32) for i in range(chunks)]
        squares = sum(jnp.sum(p * p, axis=1, keepdims=True) for p in parts)
        scale = lax.rsqrt(squares * (1.0 / (chunks * chunk)) + 1e-06)
        for i, p in enumerate(parts):
            gain = gain_ref[:, i * chunk : (i + 1) * chunk]
            out_ref[group * rows : (group + 1) * rows, i * chunk : (i + 1) * chunk] = (
                p * scale * gain
            ).astype(jnp.bfloat16)


def norm_rows(incoming, gain, groups, chunks):
    rows, chunk = incoming.shape[1:]
    shape = (groups * rows, chunks * chunk)
    return pl.pallas_call(
        functools.partial(norm_kernel, groups, chunks),
        in_specs=[pl.BlockSpec(memory_space=pltpu.VMEM)] * 2,
        out_shape=jax.ShapeDtypeStruct(shape, jnp.bfloat16),
        cost_estimate=pl.CostEstimate(
            flops=4 * shape[0] * shape[1], bytes_accessed=4 * shape[0] * shape[1], transcendentals=shape[0]
        ),
        name="norm_rows",
        interpret=INTERPRET,
    )(in_vmem(incoming), gain[None, :])


def expert_kernel(count, *refs):
    own, other = refs[:count], refs[count : 2 * count]
    gate_up, down, own_out, other_out, acc = refs[2 * count :]
    step = pl.program_id(0)
    rows = jnp.concatenate([r[...] for r in own + other], axis=0)

    @pl.when(step == 0)
    def _():
        acc[...] = jnp.zeros(acc.shape, jnp.float32)

    acc[...] += jnp.dot(rows, gate_up[...], preferred_element_type=jnp.float32)

    @pl.when(step == pl.num_programs(0) - 1)
    def _():
        width = down.shape[0]
        half = own_out.shape[0]
        gate = acc[:, :width]
        hidden = (gate / (1.0 + jnp.exp(-gate)) * acc[:, width:]).astype(jnp.bfloat16)
        part = min(512, down.shape[1])

        def columns(i, carry):
            at = pl.ds(pl.multiple_of(i * part, part), part)
            out = jnp.dot(hidden, down[:, at], preferred_element_type=jnp.float32).astype(jnp.bfloat16)
            own_out[:, at] = out[:half]
            other_out[:, at] = out[half:]
            return carry

        lax.fori_loop(0, down.shape[1] // part, columns, 0)


def expert_block(own, other, gate_up, down_weight):
    count = len(own)
    rows, width = own[0].shape
    deep = min(DEEP, width)
    total = 2 * count * rows
    block = pl.BlockSpec((rows, deep), lambda i: (0, i))
    shape = (count * rows, width)
    whole = pl.BlockSpec(shape, lambda i: (0, 0))
    out_own, out_other = pl.pallas_call(
        functools.partial(expert_kernel, count),
        grid=(width // deep,),
        in_specs=[block] * (2 * count)
        + [pl.BlockSpec((deep, gate_up.shape[1]), lambda i: (i, 0)), pl.BlockSpec(down_weight.shape, lambda i: (0, 0))],
        out_specs=[whole, whole],
        out_shape=[jax.ShapeDtypeStruct(shape, jnp.bfloat16)] * 2,
        scratch_shapes=[pltpu.VMEM((total, gate_up.shape[1]), jnp.float32)],
        cost_estimate=pl.CostEstimate(
            flops=2 * total * (gate_up.size + down_weight.size),
            bytes_accessed=2 * (gate_up.size + down_weight.size + 2 * total * width),
            transcendentals=total * down_weight.shape[0],
        ),
        interpret=INTERPRET,
    )(*own, *other, gate_up, down_weight)
    return add_rounded(out_own, swap(out_other))


def add_rounded(a, b):
    return (a.astype(jnp.float32) + b.astype(jnp.float32)).astype(jnp.bfloat16)


def last_sum_kernel(own_ref, low_a, low_b, high_a, high_b, out_ref):
    half = low_a.shape[0]
    wide = own_ref.shape[1] // 2
    for start, first, second in ((0, low_a, low_b), (half, high_a, high_b)):
        for at in range(0, half, CAP):
            rows = slice(start + at, start + at + CAP)
            whole = (
                own_ref[rows].astype(jnp.float32)
                + first[at : at + CAP].astype(jnp.float32)
                + second[at : at + CAP].astype(jnp.float32)
            )
            both = jnp.concatenate([whole[:, :wide], whole[:, wide:]], axis=0)
            out_ref[(start + at) // CAP] = both.astype(jnp.bfloat16)


def last_sum(own, low_a, low_b, high_a, high_b):
    rows, width = own.shape
    shape = (rows // CAP, 2 * CAP, width // 2)
    return pl.pallas_call(
        last_sum_kernel,
        out_shape=jax.ShapeDtypeStruct(shape, jnp.bfloat16),
        cost_estimate=pl.CostEstimate(
            flops=2 * rows * width, bytes_accessed=8 * rows * width, transcendentals=0
        ),
        name="last_sum",
        interpret=INTERPRET,
    )(own, low_a, low_b, high_a, high_b)


def combine_kernel(picked_ref, returned_ref, out_ref):
    rows, wide = out_ref.shape[0], returned_ref.shape[1]
    both = jnp.dot(picked_ref[...], returned_ref[...], preferred_element_type=jnp.float32)
    for half in range(2):
        out_ref[:, half * wide : (half + 1) * wide] = both[half * rows : (half + 1) * rows].astype(
            jnp.bfloat16
        )


def combine(picked, returned):
    shape = (picked.shape[0] // 2, 2 * returned.shape[1])
    return pl.pallas_call(
        combine_kernel,
        in_specs=[pl.BlockSpec(memory_space=pltpu.VMEM)] * 2,
        out_shape=jax.ShapeDtypeStruct(shape, jnp.bfloat16),
        cost_estimate=pl.CostEstimate(
            flops=2 * picked.shape[0] * returned.size,
            bytes_accessed=2 * (returned.size + shape[0] * shape[1]),
            transcendentals=0,
        ),
        name="combine",
        interpret=INTERPRET,
    )(picked, in_vmem(returned))


def on_device(
    queries, doc_keys, doc_values, residual, out_weight, norm_gain, expert_ids, gate_up, down_weight
):
    nx, nzlo, ny, nzhi = (lax.axis_size(a) for a in ("x", "zlo", "y", "zhi"))
    rows, width = residual.shape
    chunk = width // nx
    group = nzlo * ny
    experts = nx * nzlo

    at_x = lax.axis_index("x").astype(jnp.int32).reshape(1)
    ordered = queries.reshape(nx, group, rows, -1).transpose(1, 0, 2, 3).reshape(queries.shape)
    sent = pack(residual, expert_ids, out_weight)
    payload = lax.all_to_all(sent, "x", split_axis=0, concat_axis=0, tiled=True)
    residual_chunk, chosen = choose(payload, rows, chunk, nx, nzlo)
    context, (payload, residual_chunk, chosen) = attention(
        ordered, doc_keys, doc_values, (payload, residual_chunk, chosen)
    )
    contexts = [context] + [shift(context, "x", step) for step in X_STEPS[1:]]
    partial_rows = project(at_x, contexts, payload, chunk)
    pieces = lax.all_to_all(
        partial_rows.reshape(group, nx * rows, chunk), ("zlo", "y"), split_axis=0, concat_axis=0, tiled=True
    )
    mixed = jnp.sum(pieces.astype(jnp.float32), axis=0)
    attended_chunk = (residual_chunk.astype(jnp.float32) + mixed).astype(jnp.bfloat16)
    attended = lax.all_to_all(attended_chunk, "x", split_axis=0, concat_axis=1, tiled=True)

    outgoing = jnp.dot(chosen, attended_chunk, preferred_element_type=jnp.float32).astype(jnp.bfloat16)
    outgoing = outgoing.reshape(1, experts, nx * CAP, chunk)
    outgoing = jnp.broadcast_to(outgoing, (nzhi,) + outgoing.shape[1:]).reshape(
        nzhi * experts, nx * CAP, chunk
    )
    incoming = lax.all_to_all(outgoing, PLANE, split_axis=0, concat_axis=0, tiled=True)
    normed = norm_rows(incoming, norm_gain, nzhi * nzlo, nx)

    half = normed.shape[0] // 2
    gate_up, down_weight = gate_up[0], down_weight[0]
    from_prev, from_next = shift(normed, "y", 1), shift(normed, "y", -1)
    sum_own = expert_block([normed], [swap(normed)], gate_up, down_weight)
    far_up = shift(from_prev[:half], "y", 1)
    far_down = shift(from_next[half:], "y", -1)
    sides = [from_prev, from_next]
    sum_side = expert_block(sides, [swap(r) for r in sides], gate_up, down_weight)
    prev_low, prev_high, next_low, next_high = (sum_side[i * half : (i + 1) * half] for i in range(4))
    early_next, early_prev = shift(next_high, "y", 1), shift(prev_low, "y", -1)
    far = jnp.concatenate([far_up, far_down], axis=0)
    sum_far = expert_block([far], [swap(far)], gate_up, down_weight)
    relay_next, relay_prev = shift(sum_far[:half], "y", 1), shift(sum_far[half:], "y", -1)
    late_next = shift(add_rounded(next_low, relay_next), "y", 1)
    late_prev = shift(add_rounded(prev_high, relay_prev), "y", -1)
    summed = last_sum(sum_own, late_next, early_prev, early_next, late_prev)
    returned = lax.all_to_all(summed, PLANE, split_axis=0, concat_axis=0, tiled=True)
    own_routes = expert_ids[:, 0]
    positions = jnp.arange(rows, dtype=jnp.int32)
    slots = jnp.arange(CAP, dtype=jnp.int32)
    expert_of = (
        jnp.arange(nx, dtype=jnp.int32)[None, :] * nzlo + jnp.arange(nzlo, dtype=jnp.int32)[:, None]
    ).reshape(-1)
    own_earlier = (own_routes[:, None] == own_routes[None, :]) & (positions[:, None] > positions[None, :])
    own_rank = jnp.sum(own_earlier.astype(jnp.int32), axis=1)
    picked = (own_routes[:, None, None] == expert_of[None, :, None]) & (
        own_rank[:, None, None] == slots[None, None, :]
    )
    halves = jnp.arange(2, dtype=jnp.int32)
    picked = (halves[:, None] == halves[None, :])[:, None, None, None, :, None] & jnp.broadcast_to(
        picked[None, :, None, :, None, :], (1, rows, nzhi, nx * nzlo, 1, CAP)
    )
    expert_sum = combine(
        picked.reshape(2 * rows, -1).astype(jnp.bfloat16), returned.reshape(-1, width // 2)
    )
    return (attended, expert_sum)


def solution(mesh):
    split = Mesh(mesh.devices.reshape(4, 2, 4, 2, 4), CTX + EXP)
    return jax.shard_map(
        on_device,
        mesh=split,
        in_specs=(
            P(CTX, EXP),
            P(CTX, EXP),
            P(CTX, EXP),
            P(CTX + EXP, None),
            P(EXP, None),
            P(),
            P(CTX + EXP, None),
            P(EXP, None, CTX),
            P(EXP, CTX, None),
        ),
        out_specs=(P(CTX + EXP, None), P(CTX + EXP, None)),
        check_vma=False,
    )
```

```python
import functools

import jax
import jax.numpy as jnp
from jax import lax
from jax.experimental import pallas as pl
from jax.experimental.pallas import tpu as pltpu
from jax.sharding import Mesh
from jax.sharding import PartitionSpec as P

DH = 64
CAP = 4
CTX = ("zhi", "core")
EXP = ("x", "zlo", "y")
PLANE = ("zhi", "zlo", "x")
INTERPRET = False


DEEP = 512


def shift(value, axis, step):
    size = lax.axis_size(axis)
    return lax.ppermute(value, axis, [(i, (i + step) % size) for i in range(size)])


def swap(value):
    return shift(value, "core", 1)


def in_vmem(value):
    return value if INTERPRET else pltpu.with_memory_space_constraint(value, pltpu.VMEM)


def attend_kernel(count, first, last, *refs):
    q_ref, keys, values = refs[0], refs[1 : 1 + count], refs[1 + count : 1 + 2 * count]
    rest = refs[1 + 2 * count :]
    if not first:
        acc_in, top_in, total_in = rest[:3]
        rest = rest[3:]
    head = pl.program_id(1)
    queries = q_ref[...]
    mine = lax.broadcasted_iota(jnp.int32, queries.shape, 1) // DH == head
    own = jnp.where(mine, queries, jnp.zeros_like(queries)) * jnp.asarray(DH**-0.5, queries.dtype)
    if first:
        top = jnp.full((queries.shape[0], 1), -jnp.inf, jnp.float32)
        total = jnp.zeros((queries.shape[0], 1), jnp.float32)
        acc = jnp.zeros(queries.shape, jnp.float32)
    else:
        top = jnp.max(jnp.where(mine, top_in[...], -jnp.inf), axis=1, keepdims=True)
        total = jnp.max(jnp.where(mine, total_in[...], 0.0), axis=1, keepdims=True)
        acc = acc_in[...]
    for key, value in zip(keys, values):
        scores = lax.dot_general(
            own, key[...], (((1,), (1,)), ((), ())), preferred_element_type=jnp.float32
        )
        new_top = jnp.maximum(top, jnp.max(scores, axis=1, keepdims=True))
        decay = jnp.exp(top - new_top)
        weights = jnp.exp(scores - new_top)
        total = total * decay + jnp.sum(weights, axis=1, keepdims=True)
        acc = acc * decay + jnp.dot(
            weights.astype(jnp.bfloat16), value[...], preferred_element_type=jnp.float32
        )
        top = new_top
    if last:
        results = ((acc / total).astype(jnp.bfloat16),)
    else:
        results = (acc, jnp.broadcast_to(top, acc.shape), jnp.broadcast_to(total, acc.shape))

    @pl.when(head == 0)
    def _():
        for ref, result in zip(rest, results):
            ref[...] = result

    @pl.when(head != 0)
    def _():
        for ref, result in zip(rest, results):
            ref[...] = jnp.where(mine, result, ref[...])


def attend(queries, keys, values, state, last):
    total_rows, width = queries.shape
    rows = min(256, total_rows)
    heads = width // DH
    whole = [pl.BlockSpec(k.shape, lambda i, h: (0, 0)) for k in keys + values]
    part = pl.BlockSpec((rows, width), lambda i, h: (i, 0))
    docs = sum(k.shape[0] for k in keys)
    if last:
        shapes = [jax.ShapeDtypeStruct(queries.shape, jnp.bfloat16)]
    else:
        shapes = [jax.ShapeDtypeStruct(queries.shape, jnp.float32)] * 3
    return pl.pallas_call(
        functools.partial(attend_kernel, len(keys), not state, last),
        grid=(total_rows // rows, heads),
        in_specs=[part] + whole + [part] * len(state),
        out_specs=[part] * len(shapes),
        out_shape=shapes,
        cost_estimate=pl.CostEstimate(
            flops=4 * total_rows * docs * width,
            bytes_accessed=4 * docs * width + 14 * total_rows * width,
            transcendentals=heads * total_rows * docs,
        ),
        interpret=INTERPRET,
    )(queries, *keys, *values, *state)


def attention(queries, keys, values, early):
    near_keys = [swap(keys), shift(keys, "zhi", 1), shift(keys, "zhi", -1)]
    near_values = [swap(values), shift(values, "zhi", 1), shift(values, "zhi", -1)]
    state = attend(queries, [keys, near_keys[0]], [values, near_values[0]], [], False)
    state, early = lax.optimization_barrier((state, early))
    far_key = shift(near_keys[1], "zhi", 1)
    far_value = shift(near_values[2], "zhi", -1)
    state = attend(
        queries,
        near_keys[1:] + [swap(k) for k in near_keys[1:]],
        near_values[1:] + [swap(v) for v in near_values[1:]],
        state,
        False,
    )
    state, far_key, far_value = lax.optimization_barrier((state, far_key, far_value))
    (context,) = attend(queries, [far_key, swap(far_key)], [far_value, swap(far_value)], state, True)
    return context, early


def pack_kernel(residual_ref, ids_ref, weight_ref, out_ref):
    wide, chunk = weight_ref.shape[0], weight_ref.shape[1] // out_ref.shape[0]
    rest = out_ref.shape[2] - chunk
    rows = residual_ref.shape[0]
    ids = jnp.broadcast_to(ids_ref[...].astype(jnp.float32), (rows, rest)).astype(jnp.bfloat16)
    for part in range(out_ref.shape[0]):
        at = slice(part * chunk, (part + 1) * chunk)
        out_ref[part, :wide, :chunk] = weight_ref[:, at]
        out_ref[part, :wide, chunk:] = jnp.zeros((wide, rest), jnp.bfloat16)
        out_ref[part, wide:, :chunk] = residual_ref[:, at]
        out_ref[part, wide:, chunk:] = ids


def pack(residual, ids, weight):
    nx = lax.axis_size("x")
    shape = (nx, weight.shape[0] + residual.shape[0], weight.shape[1] // nx + 128)
    return pl.pallas_call(
        pack_kernel,
        in_specs=[pl.BlockSpec(memory_space=pltpu.VMEM)] * 3,
        out_shape=jax.ShapeDtypeStruct(shape, jnp.bfloat16),
        cost_estimate=pl.CostEstimate(
            flops=0, bytes_accessed=4 * weight.shape[0] * weight.shape[1], transcendentals=0
        ),
        name="pack",
        interpret=INTERPRET,
    )(residual, ids, weight)


def choose_kernel(nx, nzlo, got_ref, residual_ref, chosen_ref):
    rows, chunk = got_ref.shape[1], residual_ref.shape[1]
    tokens = nx * rows
    for part in range(nx):
        residual_ref[part * rows : (part + 1) * rows] = got_ref[part, :, :chunk]
    ids = [got_ref[part, :, chunk : chunk + tokens].astype(jnp.float32) for part in range(nx)]
    by_row = jnp.concatenate(ids, axis=0)
    row = lax.broadcasted_iota(jnp.int32, (tokens, tokens), 0)
    column = lax.broadcasted_iota(jnp.int32, (tokens, tokens), 1)
    by_column = jnp.sum(jnp.where(row == column, by_row, 0.0), axis=0, keepdims=True)
    earlier = (by_row == by_column) & (row // rows == column // rows) & (row < column)
    rank = jnp.sum(earlier.astype(jnp.float32), axis=0, keepdims=True)
    slots = chosen_ref.shape[0]
    row = lax.broadcasted_iota(jnp.int32, (slots, tokens), 0)
    column = lax.broadcasted_iota(jnp.int32, (slots, tokens), 1)
    plane = row // (nx * CAP)
    expert = (plane % nx * nzlo + plane // nx).astype(jnp.float32)
    chosen = (
        (by_column == expert)
        & (rank == (row % CAP).astype(jnp.float32))
        & (row // CAP % nx == column // rows)
    )
    chosen_ref[...] = chosen.astype(jnp.bfloat16)


def choose(payload, rows, chunk, nx, nzlo):
    high = payload.shape[1] // rows - 1
    shapes = [(nx * rows, chunk), (nx * nzlo * nx * CAP, nx * rows)]
    return pl.pallas_call(
        functools.partial(choose_kernel, nx, nzlo),
        grid=(1,),
        in_specs=[pl.BlockSpec((nx, rows, payload.shape[2]), lambda i: (0, high, 0))],
        out_specs=[pl.BlockSpec(shape, lambda i: (0, 0)) for shape in shapes],
        out_shape=[jax.ShapeDtypeStruct(shape, jnp.bfloat16) for shape in shapes],
        cost_estimate=pl.CostEstimate(flops=10**7, bytes_accessed=4 * shapes[0][0] * chunk, transcendentals=0),
        name="choose",
        interpret=INTERPRET,
    )(payload)


def project_kernel(chunk, payload_ref, contexts_ref, out_ref):
    nx, _, width = contexts_ref.shape
    context = jnp.concatenate([contexts_ref[i] for i in range(nx)], axis=1)
    weight = jnp.concatenate([payload_ref[i, :width, :chunk] for i in range(nx)], axis=0)
    out_ref[...] = jnp.dot(context, weight, preferred_element_type=jnp.float32).astype(jnp.bfloat16)


def project(contexts, payload, chunk):
    count, rows, width = contexts.shape
    part = min(256, rows)
    return pl.pallas_call(
        functools.partial(project_kernel, chunk),
        grid=(rows // part,),
        in_specs=[
            pl.BlockSpec(payload.shape, lambda i: (0, 0, 0)),
            pl.BlockSpec((count, part, width), lambda i: (0, i, 0)),
        ],
        out_specs=pl.BlockSpec((part, chunk), lambda i: (i, 0)),
        out_shape=jax.ShapeDtypeStruct((rows, chunk), jnp.bfloat16),
        cost_estimate=pl.CostEstimate(
            flops=2 * rows * width * count * chunk,
            bytes_accessed=2 * (rows * width * count + width * count * chunk + rows * chunk),
            transcendentals=0,
        ),
        name="project",
        interpret=INTERPRET,
    )(payload, contexts)


def norm_kernel(groups, chunks, in_ref, gain_ref, out_ref):
    rows, chunk = in_ref.shape[1:]
    for group in range(groups):
        parts = [in_ref[group * chunks + i].astype(jnp.float32) for i in range(chunks)]
        squares = sum(jnp.sum(p * p, axis=1, keepdims=True) for p in parts)
        scale = lax.rsqrt(squares * (1.0 / (chunks * chunk)) + 1e-06)
        for i, p in enumerate(parts):
            gain = gain_ref[:, i * chunk : (i + 1) * chunk]
            out_ref[group * rows : (group + 1) * rows, i * chunk : (i + 1) * chunk] = (
                p * scale * gain
            ).astype(jnp.bfloat16)


def norm_rows(incoming, gain, groups, chunks):
    rows, chunk = incoming.shape[1:]
    shape = (groups * rows, chunks * chunk)
    return pl.pallas_call(
        functools.partial(norm_kernel, groups, chunks),
        in_specs=[pl.BlockSpec(memory_space=pltpu.VMEM)] * 2,
        out_shape=jax.ShapeDtypeStruct(shape, jnp.bfloat16),
        cost_estimate=pl.CostEstimate(
            flops=4 * shape[0] * shape[1], bytes_accessed=4 * shape[0] * shape[1], transcendentals=shape[0]
        ),
        name="norm_rows",
        interpret=INTERPRET,
    )(in_vmem(incoming), gain[None, :])


def expert_kernel(count, *refs):
    own, other = refs[:count], refs[count : 2 * count]
    gate_up, down, own_out, other_out, acc = refs[2 * count :]
    width, whole = down.shape
    deep, part = min(DEEP, whole), min(512, whole)
    acc[...] = jnp.zeros(acc.shape, jnp.float32)

    def accumulate(i, carry):
        at = pl.ds(pl.multiple_of(i * deep, deep), deep)
        rows = jnp.concatenate([r[:, at] for r in own + other], axis=0)
        acc[...] += jnp.dot(rows, gate_up[at, :], preferred_element_type=jnp.float32)
        return carry

    lax.fori_loop(0, whole // deep, accumulate, 0)
    half = own_out.shape[0]
    gate = acc[:, :width]
    hidden = (gate / (1.0 + jnp.exp(-gate)) * acc[:, width:]).astype(jnp.bfloat16)

    def columns(i, carry):
        at = pl.ds(pl.multiple_of(i * part, part), part)
        out = jnp.dot(hidden, down[:, at], preferred_element_type=jnp.float32).astype(jnp.bfloat16)
        own_out[:, at] = out[:half]
        other_out[:, at] = out[half:]
        return carry

    lax.fori_loop(0, whole // part, columns, 0)


def expert_block(own, other, gate_up, down_weight):
    count = len(own)
    rows, width = own[0].shape
    total = 2 * count * rows
    shape = (count * rows, width)
    operands = [in_vmem(v) for v in (*own, *other, gate_up, down_weight)]
    out_own, out_other = pl.pallas_call(
        functools.partial(expert_kernel, count),
        in_specs=[pl.BlockSpec(memory_space=pltpu.VMEM)] * len(operands),
        out_shape=[jax.ShapeDtypeStruct(shape, jnp.bfloat16)] * 2,
        scratch_shapes=[pltpu.VMEM((total, gate_up.shape[1]), jnp.float32)],
        compiler_params=pltpu.CompilerParams(vmem_limit_bytes=24 << 20),
        cost_estimate=pl.CostEstimate(
            flops=2 * total * (gate_up.size + down_weight.size),
            bytes_accessed=2 * (gate_up.size + down_weight.size + 2 * total * width),
            transcendentals=total * down_weight.shape[0],
        ),
        interpret=INTERPRET,
    )(*operands)
    return add_rounded(out_own, swap(out_other))


def add_rounded(a, b):
    return (a.astype(jnp.float32) + b.astype(jnp.float32)).astype(jnp.bfloat16)


def last_sum_kernel(own_ref, low_a, low_b, high_a, high_b, out_ref):
    half = low_a.shape[0]
    wide = own_ref.shape[1] // 2
    for start, first, second in ((0, low_a, low_b), (half, high_a, high_b)):
        for at in range(0, half, CAP):
            rows = slice(start + at, start + at + CAP)
            whole = (
                own_ref[rows].astype(jnp.float32)
                + first[at : at + CAP].astype(jnp.float32)
                + second[at : at + CAP].astype(jnp.float32)
            )
            both = jnp.concatenate([whole[:, :wide], whole[:, wide:]], axis=0)
            out_ref[(start + at) // CAP] = both.astype(jnp.bfloat16)


def last_sum(own, low_a, low_b, high_a, high_b):
    rows, width = own.shape
    shape = (rows // CAP, 2 * CAP, width // 2)
    return pl.pallas_call(
        last_sum_kernel,
        out_shape=jax.ShapeDtypeStruct(shape, jnp.bfloat16),
        cost_estimate=pl.CostEstimate(
            flops=2 * rows * width, bytes_accessed=8 * rows * width, transcendentals=0
        ),
        name="last_sum",
        interpret=INTERPRET,
    )(own, low_a, low_b, high_a, high_b)


def combine_kernel(picked_ref, returned_ref, out_ref):
    rows, wide = out_ref.shape[0], returned_ref.shape[1]
    both = jnp.dot(picked_ref[...], returned_ref[...], preferred_element_type=jnp.float32)
    for half in range(2):
        out_ref[:, half * wide : (half + 1) * wide] = both[half * rows : (half + 1) * rows].astype(
            jnp.bfloat16
        )


def combine(picked, returned):
    shape = (picked.shape[0] // 2, 2 * returned.shape[1])
    return pl.pallas_call(
        combine_kernel,
        in_specs=[pl.BlockSpec(memory_space=pltpu.VMEM)] * 2,
        out_shape=jax.ShapeDtypeStruct(shape, jnp.bfloat16),
        cost_estimate=pl.CostEstimate(
            flops=2 * picked.shape[0] * returned.size,
            bytes_accessed=2 * (returned.size + shape[0] * shape[1]),
            transcendentals=0,
        ),
        name="combine",
        interpret=INTERPRET,
    )(picked, in_vmem(returned))


def on_device(
    queries, doc_keys, doc_values, residual, out_weight, norm_gain, expert_ids, gate_up, down_weight
):
    nx, nzlo, ny, nzhi = (lax.axis_size(a) for a in ("x", "zlo", "y", "zhi"))
    rows, width = residual.shape
    chunk = width // nx
    group = nzlo * ny
    experts = nx * nzlo

    ordered = queries.reshape(nx, group, rows, -1).transpose(1, 0, 2, 3).reshape(queries.shape)
    sent = pack(residual, expert_ids, out_weight)
    payload = lax.all_to_all(sent, "x", split_axis=0, concat_axis=0, tiled=True)
    residual_chunk, chosen = choose(payload, rows, chunk, nx, nzlo)
    context, (payload, residual_chunk, chosen) = attention(
        ordered, doc_keys, doc_values, (payload, residual_chunk, chosen)
    )
    contexts = lax.all_gather(context, "x", axis=0, tiled=False)
    partial_rows = project(contexts, payload, chunk)
    pieces = lax.all_to_all(
        partial_rows.reshape(group, nx * rows, chunk), ("zlo", "y"), split_axis=0, concat_axis=0, tiled=True
    )
    mixed = jnp.sum(pieces.astype(jnp.float32), axis=0)
    attended_chunk = (residual_chunk.astype(jnp.float32) + mixed).astype(jnp.bfloat16)
    attended = lax.all_to_all(attended_chunk, "x", split_axis=0, concat_axis=1, tiled=True)

    outgoing = jnp.dot(chosen, attended_chunk, preferred_element_type=jnp.float32).astype(jnp.bfloat16)
    outgoing = outgoing.reshape(1, experts, nx * CAP, chunk)
    outgoing = jnp.broadcast_to(outgoing, (nzhi,) + outgoing.shape[1:]).reshape(
        nzhi * experts, nx * CAP, chunk
    )
    incoming = lax.all_to_all(outgoing, PLANE, split_axis=0, concat_axis=0, tiled=True)
    normed = norm_rows(incoming, norm_gain, nzhi * nzlo, nx)

    half = normed.shape[0] // 2
    gate_up, down_weight = gate_up[0], down_weight[0]
    from_prev, from_next = shift(normed, "y", 1), shift(normed, "y", -1)
    sum_own = expert_block([normed], [swap(normed)], gate_up, down_weight)
    far_up = shift(from_prev[:half], "y", 1)
    far_down = shift(from_next[half:], "y", -1)
    sides = [from_prev, from_next]
    sum_side = expert_block(sides, [swap(r) for r in sides], gate_up, down_weight)
    prev_low, prev_high, next_low, next_high = (sum_side[i * half : (i + 1) * half] for i in range(4))
    early_next, early_prev = shift(next_high, "y", 1), shift(prev_low, "y", -1)
    far = jnp.concatenate([far_up, far_down], axis=0)
    sum_far = expert_block([far], [swap(far)], gate_up, down_weight)
    relay_next, relay_prev = shift(sum_far[:half], "y", 1), shift(sum_far[half:], "y", -1)
    late_next = shift(add_rounded(next_low, relay_next), "y", 1)
    late_prev = shift(add_rounded(prev_high, relay_prev), "y", -1)
    summed = last_sum(sum_own, late_next, early_prev, early_next, late_prev)
    returned = lax.all_to_all(summed, PLANE, split_axis=0, concat_axis=0, tiled=True)
    own_routes = expert_ids[:, 0]
    positions = jnp.arange(rows, dtype=jnp.int32)
    slots = jnp.arange(CAP, dtype=jnp.int32)
    expert_of = (
        jnp.arange(nx, dtype=jnp.int32)[None, :] * nzlo + jnp.arange(nzlo, dtype=jnp.int32)[:, None]
    ).reshape(-1)
    own_earlier = (own_routes[:, None] == own_routes[None, :]) & (positions[:, None] > positions[None, :])
    own_rank = jnp.sum(own_earlier.astype(jnp.int32), axis=1)
    picked = (own_routes[:, None, None] == expert_of[None, :, None]) & (
        own_rank[:, None, None] == slots[None, None, :]
    )
    halves = jnp.arange(2, dtype=jnp.int32)
    picked = (halves[:, None] == halves[None, :])[:, None, None, None, :, None] & jnp.broadcast_to(
        picked[None, :, None, :, None, :], (1, rows, nzhi, nx * nzlo, 1, CAP)
    )
    expert_sum = combine(
        picked.reshape(2 * rows, -1).astype(jnp.bfloat16), returned.reshape(-1, width // 2)
    )
    return (attended, expert_sum)


def solution(mesh):
    split = Mesh(mesh.devices.reshape(4, 2, 4, 2, 4), CTX + EXP)
    return jax.shard_map(
        on_device,
        mesh=split,
        in_specs=(
            P(CTX, EXP),
            P(CTX, EXP),
            P(CTX, EXP),
            P(CTX + EXP, None),
            P(EXP, None),
            P(),
            P(CTX + EXP, None),
            P(EXP, None, CTX),
            P(EXP, CTX, None),
        ),
        out_specs=(P(CTX + EXP, None), P(CTX + EXP, None)),
        check_vma=False,
    )
```
